32 devices in a mesh: wide: 8 (over y, x, core), narrow: 4 (over z).
Axes of the slice: x: 2, y: 2, z: 4, core: 2. Of those that a mesh axis runs over, the one named last changes fastest.
Arguments:
- hidden: bfloat16 [8, 256, 2048], P('wide', None, 'narrow'), may hold values from -6 to 6
- norm_gain: bfloat16 [2, 2048], replicated, may hold values from 0.25 to 1.75
- w_qkv: bfloat16 [2048, 3, 2048], P(None, None, 'narrow'), may hold values from -1 to 1
- qk_gain: float32 [2, 2048], P(None, 'narrow'), may hold values from 0.25 to 32
- w_out: bfloat16 [2048, 2048], P('narrow'), may hold values from -0.125 to 0.125
- cache: bfloat16 [2, 8, 2048, 2048], P(None, 'wide', None, 'narrow'), may hold values from -6 to 6
- lengths: int32 [8], replicated, may hold values from 1 to 2048, 8192 in all
- placing: int32 [8], replicated, may hold values from 0 to 7, each once
- routes: int32 [8, 256, 8], P('wide'), may hold values from 0 to 15, all different within a row; in each aligned block of 256 rows (0 to 255, 256 to 511, ..., all dimensions but the last counted through in order) at most 192 rows name the same one
- gate_w: float32 [8, 256, 8], P('wide'), may hold values from 0.02 to 0.3
- w_gu: bfloat16 [16, 2048, 2, 1024], P('wide', None, None, 'narrow'), may hold values from -0.125 to 0.125
- w_down: bfloat16 [16, 1024, 2048], P('wide', 'narrow'), may hold values from -0.1875 to 0.1875
Outputs:
- result: bfloat16 [8, 256, 2048], P('wide', None, 'narrow')
- new_cache: bfloat16 [2, 8, 256, 2048], P(None, 'wide', None, 'narrow')
The draws below stay inside these ranges and needn't reach their ends.
Inputs may be any that keep to these rules, and one draw needn't show every extreme that they name: `routes`: each token names 8 different experts; among the 256 tokens of one request no expert is named more than 192 times. `lengths`: some request has 2048 cached positions. Slot s holds request placing[s]; every request is held once.
All inputs are finite; a program needn't handle non-finite values.
Results may differ from the reference program's by a relative error of at most 0.013.
Values may be sent and summed in bfloat16 or wider, within the bound.
A program may use at most 128 MiB of HBM per device.

```python
import math
import jax
import jax.numpy as jnp
import numpy as np
from jax import lax

D = 2048
H = 16
HD = 128
FF = 1024
TOPK = 8
EXPERTS = 16
SPAN = 256
CACHE = 2048
REQS = 8
CAP = 192
N_NARROW = 4


def draw_hidden(key, part):
    inner = jax.random.fold_in(key, 11)
    values = jax.random.truncated_normal(inner, -6.0, 6.0, (REQS, SPAN, D), jnp.float32)
    return values.astype(jnp.bfloat16)


def draw_w_qkv(key, part):
    inner = jax.random.fold_in(key, 17)
    values = jax.random.truncated_normal(inner, -6.0, 6.0, (D, 3, H * HD), jnp.float32) * D ** (-0.5)
    return values.astype(jnp.bfloat16)


def draw_qk_gain(key, part):
    inner = jax.random.fold_in(key, 13)
    values = 1.0 + 0.15 * jax.random.truncated_normal(inner, -4.0, 4.0, (2, H * HD), jnp.float32)
    return values.astype(jnp.float32)


def shard_levels(key, shape, cuts, least, largest):
    gain = 1.0
    for axis_at, blocks in cuts:
        steps = jax.random.uniform(jax.random.fold_in(jax.random.fold_in(key, 6), axis_at), (blocks,), jnp.float32, least / len(cuts), largest / len(cuts))
        gain = gain * jnp.repeat(jnp.exp(steps), shape[axis_at] // blocks).reshape((-1,) + (1,) * (len(shape) - 1 - axis_at))
    return gain


def split_up(count, total, limit, lean):
    loads = [(1 << 20) // math.isqrt(standing ** lean) + 1 for standing in range(2, count + 1)]
    surplus, given = total - limit - (count - 1), [1] * (count - 1)
    while surplus > 0:
        free = [i for i in range(count - 1) if given[i] < limit]
        pool, left = sum([loads[i] for i in free]), surplus
        for i in free:
            extra = min(limit - given[i], max(1, left * loads[i] // pool), surplus)
            given[i] = given[i] + extra
            surplus = surplus - extra
    return np.array([limit] + given)


def uneven(own_key, amount, total, reach, slope):
    if amount == 2:
        one = jax.random.randint(own_key, (), max(1, total - reach), min(reach, total - 1) + 1)
        return jnp.stack([one, total - one])
    sizes = jnp.asarray(split_up(amount, total, reach, slope), jnp.int32)
    pairs = (amount - 1) // 2
    source_of, receiver = sizes[1:1 + 2 * pairs:2], sizes[2:2 + 2 * pairs:2]
    margin = jnp.minimum(source_of - 1, reach - receiver)
    shifted = jax.random.randint(jax.random.fold_in(own_key, 1), (pairs,), 0, 1 << 20) % (margin + 1)
    sizes = sizes.at[1:1 + 2 * pairs:2].set(source_of - shifted).at[2:2 + 2 * pairs:2].set(receiver + shifted)
    return sizes[jax.random.permutation(jax.random.fold_in(own_key, 2), amount)]


def shared_out(rng, own, number, rows, number_of, top, limit, skew):
    sequence = jax.random.permutation(rng, number_of)
    crowded, usual = portions_of(number_of, rows * top, limit, skew, True), portions_of(number_of, rows * top, limit, skew, False)
    places = jnp.arange(number_of)

    def named(sizes, turn):
        used = int((sizes > 0).sum())
        fixed = max(1, used // 4)
        passed = fixed + (places - fixed + turn * (used - fixed)) % max(1, number_of - fixed)
        return jnp.zeros((number_of,), jnp.int32).at[sequence[jnp.where(places < fixed, places, passed)]].set(jnp.asarray(sizes, jnp.int32))

    sizes = jnp.where(number % 4 == 0, named(crowded, number // 4), named(usual, number - number // 4 - 1))
    mixed = jax.random.permutation(jax.random.fold_in(own, 3), number_of)
    source_of, receiver = mixed[0:number_of // 2 * 2:2], mixed[1:number_of // 2 * 2:2]
    margin = jnp.minimum(sizes[source_of] - 1, limit - sizes[receiver]) // 2
    margin = jnp.where((source_of == sequence[0]) | (receiver == sequence[0]) | (sizes[receiver] == 0), 0, jnp.maximum(margin, 0))
    passed = jax.random.randint(jax.random.fold_in(own, 4), (number_of // 2,), 0, 1 << 20) % (margin + 1)
    sizes = sizes.at[source_of].add(-passed).at[receiver].add(passed)
    items = jnp.searchsorted(jnp.cumsum(sizes), jnp.arange(rows * top), side="right").astype(jnp.int32)
    listing = items.reshape(top, rows).T
    listing = listing[jax.random.permutation(jax.random.fold_in(own, 1), rows)]
    turn = jax.random.randint(jax.random.fold_in(own, 2), (rows, 1), 0, top)
    return jnp.take_along_axis(listing, (jnp.arange(top)[None, :] + turn) % top, axis=1)


def portions_of(amount, total, most, skew, full):
    portions = [(1 << 20) // math.isqrt(standing ** skew) + 1 for standing in range(1, amount + 1)]
    largest = most if full else min(most, max(-(-total // amount), total * portions[0] // sum(portions)))
    least = 1 if total - largest >= amount - 1 else 0
    given, surplus = [largest] + [least] * (amount - 1), total - largest - least * (amount - 1)
    while surplus > 0:
        free = [i for i in range(1, amount) if given[i] < largest] or [i for i in range(1, amount) if given[i] < most]
        pool, budget = sum([portions[i] for i in free]), surplus
        for i in free:
            addition = min(most - given[i], max(1, budget * portions[i] // pool), surplus)
            given[i] = given[i] + addition
            surplus = surplus - addition
    return np.array(given)


def scatter_about(key, extent, spread, bound, shards=(), held_as=jnp.bfloat16):
    values = jax.random.normal(key, extent, jnp.float32) * spread
    if len(shards) > 0:
        values = shard_levels(key, extent, shards, -0.22, 0.18) * values
    return jnp.clip(values, min=-bound, max=bound).astype(held_as)


def setup_inputs(seed: int = 0) -> dict:
    keys = jax.random.split(jax.random.key(seed), 13)
    hidden = draw_hidden(jax.random.fold_in(keys[12], 71), 0)
    norm_gain = jnp.clip(1.0 + 0.15 * jax.random.normal(keys[1], (2, D), jnp.float32), 0.25, 1.75).astype(jnp.bfloat16)
    w_qkv = draw_w_qkv(jax.random.fold_in(keys[12], 71), 0)
    qk_gain = draw_qk_gain(jax.random.fold_in(keys[12], 71), 0)
    w_out = scatter_about(keys[4], (H * HD, D), (H * HD) ** -0.5, 0.125, ((0, 4),))
    cache = scatter_about(keys[5], (2, REQS, CACHE, H * HD), 1.0, 6.0, ((1, 8), (3, 4)))
    lengths = uneven(keys[6], REQS, REQS * CACHE // 2, CACHE, 1).astype(jnp.int32)
    placing = jax.random.permutation(keys[7], REQS).astype(jnp.int32)
    routes_keys = jax.random.split(jax.random.fold_in(keys[8], 1), REQS * SPAN // SPAN)
    routes_turns = jax.random.permutation(jax.random.fold_in(keys[8], 3), REQS * SPAN // SPAN)
    routes = jax.vmap(lambda own, number: shared_out(jax.random.fold_in(keys[8], 2), own, number, SPAN, EXPERTS, TOPK, CAP, 1))(routes_keys, routes_turns).reshape((REQS, SPAN, TOPK))
    gate_w = jnp.clip(jnp.exp(math.log(0.3) - 2.7080503 * jax.random.uniform(keys[9], (REQS, SPAN, TOPK), jnp.float32) ** shard_levels(keys[9], (REQS, SPAN, TOPK), ((0, 8),), -0.2, 0.2)), 0.02, 0.3)
    w_gu = scatter_about(keys[10], (EXPERTS, D, 2, FF), D ** -0.5, 0.125, ((0, 8), (3, 4)))
    w_down = scatter_about(keys[11], (EXPERTS, FF, D), FF ** -0.5, 0.1875, ((0, 8), (1, 4)))
    return dict(hidden=hidden, norm_gain=norm_gain, w_qkv=w_qkv, qk_gain=qk_gain, w_out=w_out, cache=cache, lengths=lengths, placing=placing, routes=routes, gate_w=gate_w, w_gu=w_gu, w_down=w_down)


def normalize(values, gain_row):
    values = values.astype(jnp.float32)
    return values * lax.rsqrt(lax.optimization_barrier(jnp.mean(values * values, axis=-1, keepdims=True)) + 1e-05) * gain_row.astype(jnp.float32)

def rotary(values, positions):
    half_dim = values.shape[-1] // 2
    frequency = 10000.0 ** (-(jnp.arange(half_dim, dtype=jnp.float32) * (2.0 / values.shape[-1])))
    angle = positions[:, None] * frequency[None, :]
    cosine = jnp.cos(angle)[:, None, :]
    sine_part = jnp.sin(angle)[:, None, :]
    first_half = values[..., :half_dim]
    second_half = values[..., half_dim:]
    return jnp.concatenate([first_half * cosine - second_half * sine_part, second_half * cosine + first_half * sine_part], axis=-1)

def attend(pieces, norm_gain, w_qkv, qk_gain, w_out):
    tokens, keys_old, values_old, length = pieces
    span_len = tokens.shape[0]
    features = H * HD
    normed = normalize(tokens, norm_gain[0]).astype(jnp.bfloat16)
    projected = jnp.dot(normed, w_qkv.reshape(D, 3 * features), preferred_element_type=jnp.float32)
    queries = normalize(projected[:, :features], qk_gain[0])
    keys_new = normalize(projected[:, features:2 * features], qk_gain[1])
    values_new = projected[:, 2 * features:]
    positions = length.astype(jnp.float32) + jnp.arange(span_len, dtype=jnp.float32)
    queries = rotary(queries.reshape(span_len, H, HD), positions).astype(jnp.bfloat16)
    keys_new = rotary(keys_new.reshape(span_len, H, HD), positions).astype(jnp.bfloat16)
    values_new = values_new.reshape(span_len, H, HD).astype(jnp.bfloat16)
    all_keys = jnp.concatenate([keys_old.reshape(CACHE, H, HD), keys_new], 0)
    all_values = jnp.concatenate([values_old.reshape(CACHE, H, HD), values_new], 0)
    scores = jnp.einsum('thd,jhd->htj', queries.astype(jnp.float32), all_keys.astype(jnp.float32)) * HD ** (-0.5)
    key_index = jnp.arange(CACHE + span_len, dtype=jnp.int32)[None, :]
    query_index = jnp.arange(span_len, dtype=jnp.int32)[:, None]
    allowed = jnp.where(key_index < CACHE, key_index < length, key_index - CACHE <= query_index)
    scores = jnp.where(allowed[None], scores, -1e+30)
    highest = lax.optimization_barrier(jnp.max(scores, axis=-1, keepdims=True))
    exponent = jnp.exp(scores - highest)
    weights = exponent.astype(jnp.bfloat16)
    denominator = lax.optimization_barrier(jnp.sum(exponent, axis=-1))
    summed = jnp.einsum('htj,jhd->thd', weights.astype(jnp.float32), all_values.astype(jnp.float32))
    heads_out = (summed / jnp.transpose(denominator)[:, :, None]).astype(jnp.bfloat16).reshape(span_len, features)
    attention = jnp.dot(heads_out, w_out, preferred_element_type=jnp.float32)
    after = (tokens.astype(jnp.float32) + attention).astype(jnp.bfloat16)
    fresh = jnp.stack([keys_new.reshape(span_len, features), values_new.reshape(span_len, features)])
    return (after, fresh)

def reference(hidden, norm_gain, w_qkv, qk_gain, w_out, cache, lengths, placing, routes, gate_w, w_gu, w_down):
    slot_length = lengths[placing]
    after, fresh = lax.map(lambda pieces: attend(pieces, norm_gain, w_qkv, qk_gain, w_out), (hidden, cache[0], cache[1], slot_length))
    new_cache = jnp.transpose(fresh, (1, 0, 2, 3))
    requests = hidden.shape[0]
    span_len = hidden.shape[1]
    experts = w_gu.shape[0]
    routed = normalize(after, norm_gain[1]).astype(jnp.bfloat16).reshape(requests * span_len, D)
    padded = jnp.concatenate([routed, jnp.zeros((1, D), jnp.bfloat16)], 0)

    def ranks(block_routes):
        flat_routes = block_routes.reshape(-1)
        onehot = (flat_routes[:, None] == jnp.arange(experts, dtype=jnp.int32)[None, :]).astype(jnp.int32)
        return lax.optimization_barrier(jnp.sum((jnp.cumsum(onehot, 0) - onehot) * onehot, 1))
    slot_rank = jax.vmap(ranks)(routes)
    flat_routes = routes.reshape(requests, span_len * TOPK)
    owner_slot = jnp.arange(requests, dtype=jnp.int32)[:, None]
    target = flat_routes * (requests * CAP) + owner_slot * CAP + slot_rank
    token_row = owner_slot * span_len + (jnp.arange(span_len * TOPK, dtype=jnp.int32) // TOPK)[None, :]
    source_row = jnp.full((experts * requests * CAP,), requests * span_len, jnp.int32).at[target.reshape(-1)].set(token_row.reshape(-1))
    gate_table = jnp.zeros((experts * requests * CAP,), jnp.float32).at[target.reshape(-1)].set(gate_w.reshape(-1).astype(jnp.float32))
    source_row = source_row.reshape(experts, requests * CAP)
    gate_table = gate_table.reshape(experts, requests * CAP)
    groups = N_NARROW
    group_width = FF // groups

    def expert_step(accum, item):
        gate_up, down_rows, rows_used, gate_scale = item
        inputs = padded[rows_used].astype(jnp.float32)
        projected = jnp.dot(inputs, gate_up.reshape(D, 2 * FF).astype(jnp.float32))
        activated = (jax.nn.silu(projected[:, :FF]) * projected[:, FF:]).astype(jnp.bfloat16)
        parts = jnp.einsum('rnf,nfd->nrd', activated.reshape(-1, groups, group_width).astype(jnp.float32), down_rows.reshape(groups, group_width, D).astype(jnp.float32)).astype(jnp.bfloat16)
        expert_sum = lax.optimization_barrier(jnp.sum(parts.astype(jnp.float32), 0))
        return (accum.at[rows_used].add(gate_scale[:, None] * expert_sum), None)
    accum, _ = lax.scan(expert_step, jnp.zeros((requests * span_len + 1, D), jnp.float32), (w_gu, w_down, source_row, gate_table))
    result = (after.reshape(requests * span_len, D).astype(jnp.float32) + accum[:requests * span_len]).astype(jnp.bfloat16)
    return (result.reshape(requests, span_len, D), new_cache)
```

```python
import math

import jax
import jax.numpy as jnp
from jax import lax
from jax.experimental import pallas as pl
from jax.experimental.pallas import tpu as pltpu
from jax.sharding import PartitionSpec as P

HD = 128


def normalize(values, gain_row):
    values = values.astype(jnp.float32)
    return (
        values
        * lax.rsqrt(jnp.mean(values * values, axis=-1, keepdims=True) + 1e-05)
        * gain_row.astype(jnp.float32)
    )


def rotary(values, positions):
    half_dim = values.shape[-1] // 2
    frequency = 10000.0 ** (-(jnp.arange(half_dim, dtype=jnp.float32) * (2.0 / values.shape[-1])))
    angle = positions[:, None] * frequency[None, :]
    cosine = jnp.cos(angle)[:, None, :]
    sine_part = jnp.sin(angle)[:, None, :]
    first_half = values[..., :half_dim]
    second_half = values[..., half_dim:]
    return jnp.concatenate(
        [
            first_half * cosine - second_half * sine_part,
            second_half * cosine + first_half * sine_part,
        ],
        axis=-1,
    )


NH = 2
BUFFERS = 4
RAW_ROWS = 1024
VMEM_LIMIT = 60 * 1024 * 1024
INVERSE = (0, 1, 2, 3, 4, 6, 5, 7)
EARLY_HEADS = 2


def places():
    w = lax.axis_index("wide")
    z = lax.axis_index("narrow")
    c = lax.rem(w, 2)
    dx = 2 - 4 * lax.rem(lax.div(w, 2), 2)
    dy = 4 - 8 * lax.div(w, 4)
    first = dx * (1 - c) + dy * c
    second = dy * (1 - c) + dx * c
    return w, z, 1 - 2 * c, first, second


def layer_kernel(
    lengths_ref,
    placing_ref,
    hidden_ref,
    gain_ref,
    qk_gain_ref,
    routes_ref,
    gate_ref,
    w_qkv_any,
    cache_any,
    w_out_any,
    gu_any,
    down_any,
    out_ref,
    fresh_ref,
    pieces,
    w_qkv,
    cache,
    w_out,
    raw,
    gu,
    down,
    rope,
    gates_in,
    gate_rows,
    gate_cols,
    projected,
    squares,
    heads,
    stat_out,
    stat_in,
    rs_out,
    rs_in,
    after,
    after_in,
    held,
    weighted,
    sib_out,
    sib_in,
    first_out,
    first_keep,
    first_in,
    second_out,
    second_keep,
    second_in,
    z_out,
    z_in,
    total,
    loads,
    raw_loads,
    h_send,
    h_recv,
    gates_send,
    gates_recv,
    stat_send,
    stat_recv,
    rs_send,
    rs_recv,
    after_send,
    after_recv,
    send,
    recv,
    z_send,
    z_recv,
    r_send,
    r_recv,
):
    w, z, sib, first, second = places()
    span, cols = hidden_ref.shape
    width = cols * 4
    hr = span // NH
    rb = hr // 4
    inner = gu.shape[2] // 2
    experts_held = gu.shape[0]
    steps = (
        0,
        first,
        second,
        first + second,
        sib,
        sib + second,
        sib + first,
        sib + first + second,
    )
    slots = [w + step for step in steps]
    upper = lax.div(z, 2)
    order = (z, z + 1 - 2 * lax.rem(z, 2), 2 - upper, 3 - 3 * upper)
    started = []

    def remote(src, dst, send_sem, recv_sem, device):
        return pltpu.make_async_remote_copy(
            src_ref=src,
            dst_ref=dst,
            send_sem=send_sem,
            recv_sem=recv_sem,
            device_id=device,
            device_id_type=pl.DeviceIdType.MESH,
        )

    def push(src, dst, send_sem, recv_sem, device):
        copy = remote(src, dst, send_sem, recv_sem, device)
        copy.start()
        started.append(copy)
        return copy

    def arrive(dst, recv_sem):
        remote(dst, dst, r_send.at[0], recv_sem, {"wide": w + sib}).wait_recv()

    load_qkv = pltpu.make_async_copy(w_qkv_any, w_qkv, loads.at[0])
    load_cache = pltpu.make_async_copy(cache_any, cache, loads.at[1])
    load_out = pltpu.make_async_copy(w_out_any, w_out, loads.at[2])
    load_down = pltpu.make_async_copy(down_any, down, loads.at[3])
    per_expert = width // RAW_ROWS
    chunks = experts_held * per_expert

    def load_raw(i):
        e, part = i // per_expert, i % per_expert
        return pltpu.make_async_copy(
            gu_any.at[e, pl.ds(part * RAW_ROWS, RAW_ROWS)], raw.at[i % 2], raw_loads.at[i % 2]
        )

    load_qkv.start()
    load_raw(0).start()
    load_raw(1).start()

    barrier = pltpu.get_barrier_semaphore()
    for step in steps[1:]:
        pl.semaphore_signal(
            barrier, inc=1, device_id={"wide": w + step}, device_id_type=pl.DeviceIdType.MESH
        )
    for k in (1, 2, 3):
        pl.semaphore_signal(
            barrier, inc=1, device_id={"narrow": order[k]}, device_id_type=pl.DeviceIdType.MESH
        )
    for h in range(NH):
        pieces[h, z] = hidden_ref[h * hr : (h + 1) * hr]
    pl.semaphore_wait(barrier, 10)

    def hidden_push(h):
        for k in (1, 2, 3):
            push(
                hidden_ref.at[pl.ds(h * hr, hr)],
                pieces.at[h, z],
                h_send.at[h, k],
                h_recv.at[h, z],
                {"narrow": order[k]},
            )

    hidden_push(0)
    load_cache.start()
    load_out.start()
    load_down.start()

    expert = lax.broadcasted_iota(jnp.int32, gates_in.shape[1:], 0)
    table = jnp.zeros(gates_in.shape[1:], jnp.float32)
    for k in range(routes_ref.shape[0]):
        table = table + jnp.where(routes_ref[k : k + 1, :] == expert, gate_ref[k : k + 1, :], 0.0)
    gates_in[0] = table
    for r in range(1, 8):
        push(
            gates_in.at[0],
            gates_in.at[INVERSE[r]],
            gates_send.at[r],
            gates_recv.at[INVERSE[r]],
            {"wide": w + steps[r]},
        )

    length = lengths_ref[placing_ref[w]]
    lane = lax.broadcasted_iota(jnp.int32, (1, HD), 1)
    frequency = jnp.exp(
        lax.rem(lane, HD // 2).astype(jnp.float32) * (-2.0 / HD * math.log(10000.0))
    )
    positions = (length + lax.broadcasted_iota(jnp.int32, (span, 1), 0)).astype(jnp.float32)
    angle = positions * frequency
    rope[0] = jnp.cos(angle)
    rope[1] = jnp.sin(angle) * jnp.where(lane < HD // 2, -1.0, 1.0)

    def contribute(h, src, start):
        values = pieces[h, src].astype(jnp.float32)
        at = pl.ds(pl.multiple_of(src * cols, cols), cols)
        scaled = (values * gain_ref[0:1, at].astype(jnp.float32)).astype(jnp.bfloat16)
        square = jnp.sum(values * values, axis=1, keepdims=True)
        for i in range(3):
            term = jnp.dot(scaled, w_qkv[i, at, :], preferred_element_type=jnp.float32)
            projected[h, i] = term if start else projected[h, i] + term
        wide = jnp.broadcast_to(square, squares.shape[1:])
        squares[h] = wide if start else squares[h] + wide

    def hidden_rest(h):
        def rest(k, carry):
            src = jnp.where(k == 1, order[1], jnp.where(k == 2, order[2], order[3]))
            arrive(pieces.at[h, src], h_recv.at[h, src])
            contribute(h, src, False)
            return carry

        lax.fori_loop(1, 4, rest, 0)

    load_qkv.wait()
    contribute(0, z, True)

    row = lax.broadcasted_iota(jnp.int32, (256, 256), 0)
    column = lax.broadcasted_iota(jnp.int32, (256, 256), 1)
    part_them = (column == jnp.where(row < 128, 2 * row, 2 * row - 255)).astype(jnp.bfloat16)
    for i in range(chunks):
        load_raw(i).wait()

        def part(n, carry, i=i):
            at = pl.ds(pl.multiple_of(n * 128, 128), 128)
            to = pl.ds(pl.multiple_of(i % per_expert * RAW_ROWS + n * 128, 128), 128)
            both = jnp.dot(
                part_them,
                raw[i % 2, at].reshape(256, inner),
                preferred_element_type=jnp.float32,
            ).astype(jnp.bfloat16)
            gu[i // per_expert, to, 0:inner] = both[:128]
            gu[i // per_expert, to, inner : 2 * inner] = both[128:]
            return carry

        lax.fori_loop(0, RAW_ROWS // 128, part, 0)
        if i + 2 < chunks:
            load_raw(i + 2).start()

    def stats_push(h):
        scale = lax.rsqrt(squares[h, :, :1] / width + 1e-05)
        for i in range(3):
            projected[h, i] = projected[h, i] * scale
        spot = lax.broadcasted_iota(jnp.int32, (hr, 128), 1)
        both = [
            jnp.sum(projected[h, i] * projected[h, i], axis=1, keepdims=True) for i in range(2)
        ]
        sums = jnp.where(spot == 0, both[0], jnp.where(spot == 1, both[1], 0.0))
        stat_out[h] = sums.T[:8]
        for k in (1, 2, 3):
            push(
                stat_out.at[h],
                stat_in.at[h, z],
                stat_send.at[h, k],
                stat_recv.at[h, z],
                {"narrow": order[k]},
            )
        fresh_ref[1, h * hr : (h + 1) * hr] = projected[h, 2].astype(jnp.bfloat16)

    def stats_finish(h):
        totals = stat_out[h]
        for k in (1, 2, 3):
            arrive(stat_in.at[h, order[k]], stat_recv.at[h, order[k]])
            totals = totals + stat_in[h, order[k]]
        turned = jnp.concatenate([totals, jnp.zeros((120, hr), jnp.float32)], 0).T
        scales = lax.rsqrt(turned / width + 1e-05)
        for i in range(2):
            projected[h, i] = projected[h, i] * scales[:, i : i + 1] * qk_gain_ref[i : i + 1, :]

    across = (((1,), (1,)), ((), ()))
    stored = cache.shape[1]
    exponent_scale = HD ** (-0.5) * math.log2(math.e)

    def attend(h, low, high):
        rows = slice(h * hr, (h + 1) * hr)
        seen = (h + 1) * hr
        old_allowed = lax.broadcasted_iota(jnp.int32, (1, stored), 1) < length
        new_allowed = lax.broadcasted_iota(jnp.int32, (hr, seen), 1) <= h * hr + (
            lax.broadcasted_iota(jnp.int32, (hr, seen), 0)
        )

        def head(n, carry):
            at = pl.ds(pl.multiple_of(n * HD, HD), HD)
            cosine, sine = rope[0, rows], rope[1, rows]

            def turned(i):
                values = projected[h, i, :, at]
                return (values * cosine + pltpu.roll(values, HD // 2, 1) * sine).astype(
                    jnp.bfloat16
                )

            query = turned(0)
            fresh_ref[0, rows, at] = turned(1)
            old = lax.dot_general(
                query, cache[0, :, at], across, preferred_element_type=jnp.float32
            )
            new = lax.dot_general(
                query, fresh_ref[0, :seen, at], across, preferred_element_type=jnp.float32
            )
            old = jnp.where(old_allowed, old, -1e30)
            new = jnp.where(new_allowed, new, -1e30)
            highest = jnp.maximum(
                jnp.max(old, axis=1, keepdims=True), jnp.max(new, axis=1, keepdims=True)
            )
            old = jnp.exp2((old - highest) * exponent_scale)
            new = jnp.exp2((new - highest) * exponent_scale)
            denominator = jnp.sum(old, axis=1, keepdims=True) + jnp.sum(
                new, axis=1, keepdims=True
            )
            summed = jnp.dot(
                old.astype(jnp.bfloat16), cache[1, :, at], preferred_element_type=jnp.float32
            ) + jnp.dot(
                new.astype(jnp.bfloat16),
                fresh_ref[1, :seen, at],
                preferred_element_type=jnp.float32,
            )
            heads[h, :, at] = (summed / denominator).astype(jnp.bfloat16)
            return carry

        lax.fori_loop(low, high, head, 0)

    count = cols // HD

    def project(h):
        def chunk(i, carry):
            at = pl.ds(pl.multiple_of(i * cols, cols), cols)
            rs_out[h, :, :, at] = (
                jnp.dot(heads[h], w_out[:, at], preferred_element_type=jnp.float32)
                .astype(jnp.bfloat16)
                .reshape(4, rb, cols)
            )
            return carry

        lax.fori_loop(0, width // cols, chunk, 0)
        for k in (3, 2, 1):
            push(
                rs_out.at[h, order[k]],
                rs_in.at[h, z],
                rs_send.at[h, k],
                rs_recv.at[h, z],
                {"narrow": order[k]},
            )

    def columns(k):
        return pl.ds(pl.multiple_of(lax.rem(z + k, 4) * cols, cols), cols)

    def finish_after(h):
        added = rs_out[h, z].astype(jnp.float32)
        for k in (1, 2, 3):
            arrive(rs_in.at[h, order[k]], rs_recv.at[h, order[k]])
            added = added + rs_in[h, order[k]].astype(jnp.float32)
        own = pl.ds(pl.multiple_of(z * rb, rb), rb)
        tokens = jnp.concatenate([pieces[h, i, own, :] for i in range(4)], 1)
        rounded = (tokens.astype(jnp.float32) + added).astype(jnp.bfloat16)
        after[h] = rounded
        values = rounded.astype(jnp.float32)
        mean = jnp.mean(values * values, axis=1, keepdims=True)
        held[h, z, w] = (
            values * lax.rsqrt(mean + 1e-05) * gain_ref[1:2, :].astype(jnp.float32)
        ).astype(jnp.bfloat16)

    def after_push(h):
        for k in (1, 3, 2):
            push(
                after.at[h, :, columns(k)],
                after_in.at[h, k],
                after_send.at[h, k],
                after_recv.at[h, k],
                {"narrow": lax.rem(z + k, 4)},
            )

    def gate_columns():
        for r in range(1, 8):
            arrive(gates_in.at[r], gates_recv.at[r])
        gate_rows[...] = jnp.zeros_like(gate_rows)
        for r in range(8):
            for j in range(experts_held):
                at = r * experts_held + j
                gate_rows[at : at + 1, :] = jnp.sum(
                    jnp.where(expert == w * experts_held + j, gates_in[r], 0.0),
                    axis=0,
                    keepdims=True,
                )
        gate_cols[...] = gate_rows[...].T

    pushed = []

    def push_rows(slot, n, role, step):
        h, k = n // 4, n % 4
        ref = held.at[h, order[k], slot]
        push(ref, ref, send.at[len(pushed)], recv.at[role, n], {"wide": w + step})
        pushed.append(n)

    def arrive_rows(role, n):
        h, k = n // 4, n % 4
        arrive(held.at[h, order[k], slots[role]], recv.at[role, n])

    def along(h, src, way):
        ref = held.at[h, src, w]
        return remote(
            ref,
            ref,
            z_send.at[h, (way + 1) // 2, src],
            z_recv.at[h, src],
            {"narrow": lax.rem(z + way + 4, 4)},
        )

    def sends(src, way):
        return (src <= z) & (z < 3) if way > 0 else (src >= z) & (z > 0)

    def pass_on(h, src):
        for way in (1, -1):

            @pl.when(sends(src, way))
            def _(way=way):
                along(h, src, way).start()

    def expert_rows(n):
        h, g = n // 4, order[n % 4]
        inputs = jnp.concatenate([held[h, g, slot] for slot in slots], 0)
        weights = gate_cols[pl.ds(pl.multiple_of(h * hr + g * rb, rb), rb), :]
        lanes = lax.broadcasted_iota(jnp.int32, weights.shape, 1)

        def one(j, carry):
            scale = jnp.concatenate(
                [
                    jnp.sum(
                        jnp.where(lanes == r * experts_held + j, weights, 0.0),
                        axis=1,
                        keepdims=True,
                    )
                    for r in range(8)
                ],
                0,
            )
            both = jnp.dot(inputs, gu[j], preferred_element_type=jnp.float32)
            gate = both[:, :inner]
            active = gate / (1.0 + jnp.exp(-gate)) * both[:, inner:] * scale
            weighted[h, :, g, :, pl.ds(pl.multiple_of(j * inner, inner), inner)] = active.astype(
                jnp.bfloat16
            ).reshape(8, rb, inner)
            return carry

        lax.fori_loop(0, experts_held, one, 0)

    turns = (2, 1, 3, 0)
    units = 4 * NH

    def product(m, low):
        h, k = m // 4, turns[m % 4]
        values = weighted[h, low : low + 4].reshape(4 * hr, experts_held * inner)
        return jnp.dot(
            values, down[:, columns(k)], preferred_element_type=jnp.float32
        ).reshape(4, hr, cols)

    sib_copies = {}

    def stage_sib(m):
        if m >= BUFFERS:
            sib_copies[m - BUFFERS].wait_send()
        sib_out[m % BUFFERS] = product(m, 4).astype(jnp.bfloat16)
        copy = remote(
            sib_out.at[m % BUFFERS], sib_in.at[m], r_send.at[m], r_recv.at[m], {"wide": w + sib}
        )
        copy.start()
        sib_copies[m] = copy

    def stage_first(m):
        value = product(m, 0)
        arrive(sib_in.at[m], r_recv.at[m])
        for spot, r in ((0, 1), (1, 3)):
            first_out[m, spot] = (value[r] + sib_in[m, r].astype(jnp.float32)).astype(jnp.bfloat16)
        at = units + m
        push(first_out.at[m], first_in.at[m], r_send.at[at], r_recv.at[at], {"wide": w + first})
        for spot, r in ((0, 0), (1, 2)):
            first_keep[m % 2, spot] = value[r] + sib_in[m, r].astype(jnp.float32)

    def stage_second(m):
        at = units + m
        arrive(first_in.at[m], r_recv.at[at])
        second_out[m] = (first_keep[m % 2, 1] + first_in[m, 1].astype(jnp.float32)).astype(
            jnp.bfloat16
        )
        at = 2 * units + m
        push(second_out.at[m], second_in.at[m], r_send.at[at], r_recv.at[at], {"wide": w + second})
        second_keep[m % 2] = first_keep[m % 2, 0] + first_in[m, 0].astype(jnp.float32)

    def stage_along(m):
        h, k = m // 4, turns[m % 4]
        at = 2 * units + m
        arrive(second_in.at[m], r_recv.at[at])
        value = second_keep[m % 2] + second_in[m].astype(jnp.float32)
        if k:
            z_out[m] = value.astype(jnp.bfloat16)
            at = 3 * units + m
            push(
                z_out.at[m],
                z_in.at[m],
                r_send.at[at],
                r_recv.at[at],
                {"narrow": lax.rem(z + k, 4)},
            )
        else:
            total[h] = value

    def finish(h):
        for k in (1, 2, 3):
            arrive(after_in.at[h, k], after_recv.at[h, k])
        for m in range(4 * h, 4 * h + 3):
            arrive(z_in.at[m], r_recv.at[3 * units + m])
            total[h] = total[h] + z_in[m].astype(jnp.float32)
        for k in range(4):
            group = lax.rem(z + 4 - k, 4)
            block = pl.ds(pl.multiple_of(group * rb, rb), rb)
            to = pl.ds(pl.multiple_of(h * hr + group * rb, rb), rb)
            own = after_in[h, k] if k else after[h, :, columns(0)]
            out_ref[to, :] = (total[h, block, :] + own.astype(jnp.float32)).astype(jnp.bfloat16)

    hidden_rest(0)
    hidden_push(1)
    stats_push(0)
    contribute(1, z, True)
    stats_finish(0)
    load_cache.wait()
    attend(0, 0, count)
    load_out.wait()
    project(0)
    hidden_rest(1)
    stats_push(1)
    gate_columns()
    stats_finish(1)
    attend(1, 0, EARLY_HEADS)
    finish_after(0)

    lead = 7
    for t in range(lead + units + 3):
        if t < units:
            h, k = t // 4, t % 4
            if h == 1 and k == 0:
                finish_after(1)
            if k == 0:
                pass_on(h, z)
            push_rows(w, t, 1, first)
            push_rows(w, t, 2, second)
            push_rows(w, t, 4, sib)
            if k == 0:
                after_push(h)
            if k < 3:
                src = order[k + 1]
                arrive(held.at[h, src, w], z_recv.at[h, src])
                pass_on(h, src)
        if 1 <= t < units + 1:
            n = t - 1
            arrive_rows(1, n)
            push_rows(slots[1], n, 3, second)
            push_rows(slots[1], n, 5, sib)
            arrive_rows(2, n)
            push_rows(slots[2], n, 6, sib)
        if 2 <= t < units + 2:
            n = t - 2
            arrive_rows(3, n)
            push_rows(slots[3], n, 7, sib)
        if t == 0:
            attend(1, EARLY_HEADS, count)
            project(1)
        if t == 3:
            load_down.wait()
        if lead <= t < lead + units:
            stage_sib(t - lead)
        if lead + 1 <= t < lead + units + 1:
            stage_first(t - lead - 1)
        if 3 <= t < units + 3:
            n = t - 3
            for role in (4, 5, 6, 7):
                arrive_rows(role, n)
            expert_rows(n)
        if lead + 2 <= t < lead + units + 2:
            stage_second(t - lead - 2)
        if lead + 3 <= t:
            stage_along(t - lead - 3)
        if t == lead + 8:
            finish(0)
    finish(1)
    for copy in started:
        copy.wait_send()
    for m in range(units - BUFFERS, units):
        sib_copies[m].wait_send()
    for h in range(NH):
        for src in order:
            for way in (1, -1):

                @pl.when(sends(src, way))
                def _(h=h, src=src, way=way):
                    along(h, src, way).wait_send()


def layer_by_copies(
    hidden, norm_gain, w_qkv, qk_gain, w_out, cache, lengths, placing, routes, gate_w, w_gu, w_down
):
    _, span, cols = hidden.shape
    width = cols * 4
    held, _, _, inner = w_gu.shape
    experts = held * 8
    hr, rb = span // NH, span // NH // 4
    units = 4 * NH
    half, full = jnp.bfloat16, jnp.float32
    vmem = pl.BlockSpec(memory_space=pltpu.VMEM)
    smem = pl.BlockSpec(memory_space=pltpu.SMEM)
    anywhere = pl.BlockSpec(memory_space=pl.ANY)
    dma = pltpu.SemaphoreType.DMA
    scratch = pltpu.VMEM
    result, fresh = pl.pallas_call(
        layer_kernel,
        out_shape=(
            jax.ShapeDtypeStruct((span, cols), half),
            jax.ShapeDtypeStruct((2, span, cols), half),
        ),
        in_specs=[smem] * 2 + [vmem] * 5 + [anywhere] * 5,
        out_specs=(vmem, vmem),
        scratch_shapes=[
            scratch((NH, 4, hr, cols), half),
            scratch((3, width, cols), half),
            scratch((2,) + cache.shape[2:], half),
            scratch(w_out.shape, half),
            scratch((2, RAW_ROWS, 2, inner), half),
            scratch((held, width, 2 * inner), half),
            scratch((held * inner, width), half),
            scratch((2, span, HD), full),
            scratch((8, experts, span), full),
            scratch((128, span), full),
            scratch((span, 128), full),
            scratch((NH, 3, hr, cols), full),
            scratch((NH, hr, 128), full),
            scratch((NH, hr, cols), half),
            scratch((NH, 8, hr), full),
            scratch((NH, 4, 8, hr), full),
            scratch((NH, 4, rb, width), half),
            scratch((NH, 4, rb, width), half),
            scratch((NH, rb, width), half),
            scratch((NH, 4, rb, cols), half),
            scratch((NH, 4, 8, rb, width), half),
            scratch((NH, 8, 4, rb, held * inner), half),
            scratch((BUFFERS, 4, hr, cols), half),
            scratch((units, 4, hr, cols), half),
            scratch((units, 2, hr, cols), half),
            scratch((2, 2, hr, cols), full),
            scratch((units, 2, hr, cols), half),
            scratch((units, hr, cols), half),
            scratch((2, hr, cols), full),
            scratch((units, hr, cols), half),
            scratch((units, hr, cols), half),
            scratch((units, hr, cols), half),
            scratch((NH, hr, cols), full),
            dma((4,)),
            dma((2,)),
            dma((NH, 4)),
            dma((NH, 4)),
            dma((8,)),
            dma((8,)),
            dma((NH, 4)),
            dma((NH, 4)),
            dma((NH, 4)),
            dma((NH, 4)),
            dma((NH, 4)),
            dma((NH, 4)),
            dma((7 * units,)),
            dma((8, units)),
            dma((NH, 2, 4)),
            dma((NH, 4)),
            dma((4 * units,)),
            dma((4 * units,)),
        ],
        compiler_params=pltpu.CompilerParams(
            collective_id=0, has_side_effects=True, vmem_limit_bytes=VMEM_LIMIT
        ),
        name="layer",
    )(
        lengths,
        placing,
        hidden[0],
        norm_gain,
        qk_gain,
        jnp.transpose(routes[0]),
        jnp.transpose(gate_w[0]),
        jnp.transpose(w_qkv, (1, 0, 2)),
        cache[:, 0],
        w_out,
        w_gu,
        w_down.reshape(held * inner, width),
    )
    return result[None], fresh[:, None]


def router_table(routes, gate_w, experts):
    named = routes[:, :, None] == jnp.arange(experts, dtype=jnp.int32)[None, None, :]
    return jnp.sum(jnp.where(named, gate_w[:, :, None], 0.0), axis=1)


def experts_by_collectives(after_rows, gain, routes, gate_w, w_gu, w_down):
    position = lax.axis_index("wide")
    column = lax.axis_index("narrow")
    wide_size = lax.axis_size("wide")
    narrow = lax.axis_size("narrow")
    rows, full_width = after_rows.shape
    span_len, share_cols = rows * narrow, full_width // narrow
    after_all = lax.all_gather(after_rows, ("wide", "narrow"), axis=0, tiled=True)
    after_own = lax.dynamic_slice(
        after_all, (position * span_len, column * share_cols), (span_len, share_cols)
    )
    routed = normalize(after_all, gain).astype(jnp.bfloat16)
    held_experts = w_gu.shape[0]
    inner_cols = w_gu.shape[3]
    experts = held_experts * wide_size
    table = router_table(routes, gate_w, experts)
    table = lax.all_gather(table, "wide", axis=0, tiled=True)
    scale = lax.dynamic_slice_in_dim(table, position * held_experts, held_experts, 1)
    pieces = []
    for j in range(held_experts):
        gate_up = jnp.dot(
            routed,
            w_gu[j].reshape(full_width, 2 * inner_cols),
            preferred_element_type=jnp.float32,
        )
        activated = jax.nn.silu(gate_up[:, :inner_cols]) * gate_up[:, inner_cols:]
        pieces.append((activated * scale[:, j : j + 1]).astype(jnp.bfloat16))
    weighted = jnp.concatenate(pieces, 1)
    combined = jnp.dot(
        weighted,
        w_down.reshape(held_experts * inner_cols, full_width),
        preferred_element_type=jnp.float32,
    ).astype(jnp.bfloat16)
    combined = lax.psum_scatter(combined, "wide", scatter_dimension=0, tiled=True)
    expert_out = lax.psum_scatter(
        combined, "narrow", scatter_dimension=1, tiled=True
    ).astype(jnp.float32)
    return (after_own.astype(jnp.float32) + expert_out).astype(jnp.bfloat16)

def per_device(
    hidden, norm_gain, w_qkv, qk_gain, w_out, cache, lengths, placing, routes, gate_w, w_gu, w_down
):
    narrow = lax.axis_size("narrow")
    column = lax.axis_index("narrow")
    position = lax.axis_index("wide")
    span_len = hidden.shape[1]
    share_cols = hidden.shape[2]
    full_width = share_cols * narrow
    tokens = lax.all_gather(hidden[0], "narrow", axis=1, tiled=True)
    normed = normalize(tokens, norm_gain[0]).astype(jnp.bfloat16)
    local_cols = w_qkv.shape[2]
    projected = jnp.dot(
        normed, w_qkv.reshape(full_width, 3 * local_cols), preferred_element_type=jnp.float32
    )
    queries = projected[:, :local_cols]
    keys_new = projected[:, local_cols : 2 * local_cols]
    values_new = projected[:, 2 * local_cols :]
    squares = lax.psum((jnp.sum(queries * queries, -1), jnp.sum(keys_new * keys_new, -1)), "narrow")
    features = local_cols * narrow
    queries = queries * lax.rsqrt(squares[0][:, None] / features + 1e-05) * qk_gain[0]
    keys_new = keys_new * lax.rsqrt(squares[1][:, None] / features + 1e-05) * qk_gain[1]
    head_count = local_cols // HD
    length = lengths[placing[position]]
    positions = length.astype(jnp.float32) + jnp.arange(span_len, dtype=jnp.float32)
    queries = rotary(queries.reshape(span_len, head_count, HD), positions).astype(jnp.bfloat16)
    keys_new = rotary(keys_new.reshape(span_len, head_count, HD), positions).astype(jnp.bfloat16)
    values_new = values_new.reshape(span_len, head_count, HD).astype(jnp.bfloat16)
    stored = cache.shape[2]
    all_keys = jnp.concatenate([cache[0, 0].reshape(stored, head_count, HD), keys_new], 0)
    all_values = jnp.concatenate([cache[1, 0].reshape(stored, head_count, HD), values_new], 0)
    scores = jnp.einsum(
        "thd,jhd->htj", queries, all_keys, preferred_element_type=jnp.float32
    ) * HD ** (-0.5)
    key_index = jnp.arange(stored + span_len, dtype=jnp.int32)[None, :]
    query_index = jnp.arange(span_len, dtype=jnp.int32)[:, None]
    allowed = jnp.where(key_index < stored, key_index < length, key_index - stored <= query_index)
    scores = jnp.where(allowed[None], scores, -1e30)
    highest = jnp.max(scores, axis=-1, keepdims=True)
    exponent = jnp.exp(scores - highest)
    weights = exponent.astype(jnp.bfloat16)
    denominator = jnp.sum(exponent, axis=-1)
    summed = jnp.einsum("htj,jhd->thd", weights, all_values, preferred_element_type=jnp.float32)
    heads_out = (
        (summed / jnp.transpose(denominator)[:, :, None])
        .astype(jnp.bfloat16)
        .reshape(span_len, local_cols)
    )
    partial_out = jnp.dot(heads_out, w_out, preferred_element_type=jnp.float32)
    rows = span_len // narrow
    attention = lax.psum_scatter(
        partial_out.astype(jnp.bfloat16), "narrow", scatter_dimension=0, tiled=True
    ).astype(jnp.float32)
    own_rows = lax.dynamic_slice_in_dim(tokens, column * rows, rows, 0)
    after_rows = (own_rows.astype(jnp.float32) + attention).astype(jnp.bfloat16)
    result = experts_by_collectives(
        after_rows, norm_gain[1], routes[0], gate_w[0], w_gu, w_down
    )[None]
    fresh = jnp.stack(
        [keys_new.reshape(span_len, local_cols), values_new.reshape(span_len, local_cols)]
    )[:, None]
    return (result, fresh)


def solution(mesh):
    placed = (
        P("wide", None, "narrow"),
        P(),
        P(None, None, "narrow"),
        P(None, "narrow"),
        P("narrow", None),
        P(None, "wide", None, "narrow"),
        P(),
        P(),
        P("wide", None, None),
        P("wide", None, None),
        P("wide", None, None, "narrow"),
        P("wide", "narrow", None),
    )
    by_copies = mesh.shape["wide"] == 8 and mesh.shape["narrow"] == 4
    return jax.shard_map(
        layer_by_copies if by_copies else per_device,
        mesh=mesh,
        in_specs=placed,
        out_specs=(P("wide", None, "narrow"), P(None, "wide", None, "narrow")),
        check_vma=False,
    )
```

```python
import math

import jax
import jax.numpy as jnp
from jax import lax
from jax.experimental import pallas as pl
from jax.experimental.pallas import tpu as pltpu
from jax.sharding import PartitionSpec as P

HD = 128


def normalize(values, gain_row):
    values = values.astype(jnp.float32)
    return (
        values
        * lax.rsqrt(jnp.mean(values * values, axis=-1, keepdims=True) + 1e-05)
        * gain_row.astype(jnp.float32)
    )


def rotary(values, positions):
    half_dim = values.shape[-1] // 2
    frequency = 10000.0 ** (-(jnp.arange(half_dim, dtype=jnp.float32) * (2.0 / values.shape[-1])))
    angle = positions[:, None] * frequency[None, :]
    cosine = jnp.cos(angle)[:, None, :]
    sine_part = jnp.sin(angle)[:, None, :]
    first_half = values[..., :half_dim]
    second_half = values[..., half_dim:]
    return jnp.concatenate(
        [
            first_half * cosine - second_half * sine_part,
            second_half * cosine + first_half * sine_part,
        ],
        axis=-1,
    )


NH = 2
BUFFERS = 4
RAW_ROWS = 1024
VMEM_LIMIT = 60 * 1024 * 1024
INVERSE = (0, 1, 2, 3, 4, 6, 5, 7)
EARLY_HEADS = 2


def places():
    w = lax.axis_index("wide")
    z = lax.axis_index("narrow")
    c = lax.rem(w, 2)
    dx = 2 - 4 * lax.rem(lax.div(w, 2), 2)
    dy = 4 - 8 * lax.div(w, 4)
    first = dx * (1 - c) + dy * c
    second = dy * (1 - c) + dx * c
    return w, z, 1 - 2 * c, first, second


def layer_kernel(
    lengths_ref,
    placing_ref,
    hidden_ref,
    gain_ref,
    qk_gain_ref,
    routes_ref,
    gate_ref,
    w_qkv_any,
    cache_any,
    w_out_any,
    gu_any,
    down_any,
    out_ref,
    fresh_ref,
    pieces,
    w_qkv,
    cache,
    w_out,
    raw,
    gu,
    down,
    rope,
    gates_in,
    gate_rows,
    gate_cols,
    projected,
    squares,
    heads,
    stat_out,
    stat_in,
    partial,
    rs_out,
    rs_in,
    after,
    after_in,
    held,
    weighted,
    sib_out,
    sib_in,
    first_out,
    first_keep,
    first_in,
    second_out,
    second_keep,
    second_in,
    z_out,
    z_in,
    total,
    loads,
    raw_loads,
    h_send,
    h_recv,
    gates_send,
    gates_recv,
    stat_send,
    stat_recv,
    rs_send,
    rs_recv,
    after_send,
    after_recv,
    send,
    recv,
    z_send,
    z_recv,
    r_send,
    r_recv,
):
    w, z, sib, first, second = places()
    span, cols = hidden_ref.shape
    width = cols * 4
    hr = span // NH
    rb = hr // 4
    inner = gu.shape[2] // 2
    experts_held = gu.shape[0]
    steps = (
        0,
        first,
        second,
        first + second,
        sib,
        sib + second,
        sib + first,
        sib + first + second,
    )
    slots = [w + step for step in steps]
    upper = lax.div(z, 2)
    order = (z, z + 1 - 2 * lax.rem(z, 2), 2 - upper, 3 - 3 * upper)
    started = []

    def remote(src, dst, send_sem, recv_sem, device):
        return pltpu.make_async_remote_copy(
            src_ref=src,
            dst_ref=dst,
            send_sem=send_sem,
            recv_sem=recv_sem,
            device_id=device,
            device_id_type=pl.DeviceIdType.MESH,
        )

    def push(src, dst, send_sem, recv_sem, device):
        copy = remote(src, dst, send_sem, recv_sem, device)
        copy.start()
        started.append(copy)
        return copy

    def arrive(dst, recv_sem):
        remote(dst, dst, r_send.at[0], recv_sem, {"wide": w + sib}).wait_recv()

    load_qkv = pltpu.make_async_copy(w_qkv_any, w_qkv, loads.at[0])
    load_cache = pltpu.make_async_copy(cache_any, cache, loads.at[1])
    load_out = pltpu.make_async_copy(w_out_any, w_out, loads.at[2])
    load_down = pltpu.make_async_copy(down_any, down, loads.at[3])
    per_expert = width // RAW_ROWS
    chunks = experts_held * per_expert

    def load_raw(i):
        e, part = i // per_expert, i % per_expert
        return pltpu.make_async_copy(
            gu_any.at[e, pl.ds(part * RAW_ROWS, RAW_ROWS)], raw.at[i % 2], raw_loads.at[i % 2]
        )

    load_qkv.start()
    load_raw(0).start()
    load_raw(1).start()

    barrier = pltpu.get_barrier_semaphore()
    for step in steps[1:]:
        pl.semaphore_signal(
            barrier, inc=1, device_id={"wide": w + step}, device_id_type=pl.DeviceIdType.MESH
        )
    for k in (1, 2, 3):
        pl.semaphore_signal(
            barrier, inc=1, device_id={"narrow": order[k]}, device_id_type=pl.DeviceIdType.MESH
        )
    for h in range(NH):
        pieces[h, z] = hidden_ref[h * hr : (h + 1) * hr]
    pl.semaphore_wait(barrier, 10)

    def hop(buffer, send_sems, recv_sems, src, way):
        return remote(
            buffer,
            buffer,
            send_sems.at[(way + 1) // 2, src],
            recv_sems.at[src],
            {"narrow": lax.rem(z + way + 4, 4)},
        )

    def sends(src, way):
        return (src <= z) & (z < 3) if way > 0 else (src >= z) & (z > 0)

    def hidden_hop(h, src, way):
        return hop(pieces.at[h, src], h_send.at[h], h_recv.at[h], src, way)

    def hidden_pass(h, src):
        for way in (1, -1):

            @pl.when(sends(src, way))
            def _(way=way):
                hidden_hop(h, src, way).start()

    hidden_pass(0, z)
    load_cache.start()
    load_out.start()
    load_down.start()

    expert = lax.broadcasted_iota(jnp.int32, gates_in.shape[1:], 0)
    table = jnp.zeros(gates_in.shape[1:], jnp.float32)
    for k in range(routes_ref.shape[0]):
        table = table + jnp.where(routes_ref[k : k + 1, :] == expert, gate_ref[k : k + 1, :], 0.0)
    gates_in[0] = table
    for r in range(1, 8):
        push(
            gates_in.at[0],
            gates_in.at[INVERSE[r]],
            gates_send.at[r],
            gates_recv.at[INVERSE[r]],
            {"wide": w + steps[r]},
        )

    length = lengths_ref[placing_ref[w]]
    lane = lax.broadcasted_iota(jnp.int32, (1, HD), 1)
    frequency = jnp.exp(
        lax.rem(lane, HD // 2).astype(jnp.float32) * (-2.0 / HD * math.log(10000.0))
    )
    positions = (length + lax.broadcasted_iota(jnp.int32, (span, 1), 0)).astype(jnp.float32)
    angle = positions * frequency
    rope[0] = jnp.cos(angle)
    rope[1] = jnp.sin(angle) * jnp.where(lane < HD // 2, -1.0, 1.0)

    def contribute(h, src, start):
        values = pieces[h, src].astype(jnp.float32)
        at = pl.ds(pl.multiple_of(src * cols, cols), cols)
        scaled = (values * gain_ref[0:1, at].astype(jnp.float32)).astype(jnp.bfloat16)
        square = jnp.sum(values * values, axis=1, keepdims=True)
        for i in range(3):
            term = jnp.dot(scaled, w_qkv[i, at, :], preferred_element_type=jnp.float32)
            projected[h, i] = term if start else projected[h, i] + term
        wide = jnp.broadcast_to(square, squares.shape[1:])
        squares[h] = wide if start else squares[h] + wide

    def hidden_step(h, k):
        arrive(pieces.at[h, order[k]], h_recv.at[h, order[k]])
        hidden_pass(h, order[k])
        contribute(h, order[k], False)

    load_qkv.wait()
    contribute(0, z, True)

    row = lax.broadcasted_iota(jnp.int32, (256, 256), 0)
    column = lax.broadcasted_iota(jnp.int32, (256, 256), 1)
    part_them = (column == jnp.where(row < 128, 2 * row, 2 * row - 255)).astype(jnp.bfloat16)

    def part_chunk(i):
        load_raw(i).wait()

        def part(n, carry):
            at = pl.ds(pl.multiple_of(n * 128, 128), 128)
            to = pl.ds(pl.multiple_of(i % per_expert * RAW_ROWS + n * 128, 128), 128)
            both = jnp.dot(
                part_them,
                raw[i % 2, at].reshape(256, inner),
                preferred_element_type=jnp.float32,
            ).astype(jnp.bfloat16)
            gu[i // per_expert, to, 0:inner] = both[:128]
            gu[i // per_expert, to, inner : 2 * inner] = both[128:]
            return carry

        lax.fori_loop(0, RAW_ROWS // 128, part, 0)
        if i + 2 < chunks:
            load_raw(i + 2).start()

    def stats_push(h):
        scale = lax.rsqrt(squares[h, :, :1] / width + 1e-05)
        for i in range(3):
            projected[h, i] = projected[h, i] * scale
        spot = lax.broadcasted_iota(jnp.int32, (hr, 128), 1)
        both = [
            jnp.sum(projected[h, i] * projected[h, i], axis=1, keepdims=True) for i in range(2)
        ]
        sums = jnp.where(spot == 0, both[0], jnp.where(spot == 1, both[1], 0.0))
        stat_out[h] = sums.T[:8]
        for k in (1, 2, 3):
            push(
                stat_out.at[h],
                stat_in.at[h, z],
                stat_send.at[h, k],
                stat_recv.at[h, z],
                {"narrow": order[k]},
            )
        fresh_ref[1, h * hr : (h + 1) * hr] = projected[h, 2].astype(jnp.bfloat16)

    def stats_finish(h):
        totals = stat_out[h]
        for k in (1, 2, 3):
            arrive(stat_in.at[h, order[k]], stat_recv.at[h, order[k]])
            totals = totals + stat_in[h, order[k]]
        turned = jnp.concatenate([totals, jnp.zeros((120, hr), jnp.float32)], 0).T
        scales = lax.rsqrt(turned / width + 1e-05)
        for i in range(2):
            projected[h, i] = projected[h, i] * scales[:, i : i + 1] * qk_gain_ref[i : i + 1, :]

    across = (((1,), (1,)), ((), ()))
    stored = cache.shape[1]
    exponent_scale = HD ** (-0.5) * math.log2(math.e)

    def attend(h, low, high):
        rows = slice(h * hr, (h + 1) * hr)
        seen = (h + 1) * hr
        old_allowed = lax.broadcasted_iota(jnp.int32, (1, stored), 1) < length
        new_allowed = lax.broadcasted_iota(jnp.int32, (hr, seen), 1) <= h * hr + (
            lax.broadcasted_iota(jnp.int32, (hr, seen), 0)
        )

        def head(n, carry):
            at = pl.ds(pl.multiple_of(n * HD, HD), HD)
            cosine, sine = rope[0, rows], rope[1, rows]

            def turned(i):
                values = projected[h, i, :, at]
                return (values * cosine + pltpu.roll(values, HD // 2, 1) * sine).astype(
                    jnp.bfloat16
                )

            query = turned(0)
            fresh_ref[0, rows, at] = turned(1)
            old = lax.dot_general(
                query, cache[0, :, at], across, preferred_element_type=jnp.float32
            )
            new = lax.dot_general(
                query, fresh_ref[0, :seen, at], across, preferred_element_type=jnp.float32
            )
            old = jnp.where(old_allowed, old, -1e30)
            new = jnp.where(new_allowed, new, -1e30)
            highest = jnp.maximum(
                jnp.max(old, axis=1, keepdims=True), jnp.max(new, axis=1, keepdims=True)
            )
            old = jnp.exp2((old - highest) * exponent_scale)
            new = jnp.exp2((new - highest) * exponent_scale)
            denominator = jnp.sum(old, axis=1, keepdims=True) + jnp.sum(
                new, axis=1, keepdims=True
            )
            summed = jnp.dot(
                old.astype(jnp.bfloat16), cache[1, :, at], preferred_element_type=jnp.float32
            ) + jnp.dot(
                new.astype(jnp.bfloat16),
                fresh_ref[1, :seen, at],
                preferred_element_type=jnp.float32,
            )
            heads[h, :, at] = (summed / denominator).astype(jnp.bfloat16)
            return carry

        lax.fori_loop(low, high, head, 0)

    count = cols // HD

    def project(h):
        def chunk(i, carry):
            at = pl.ds(pl.multiple_of(i * cols, cols), cols)
            partial[h, :, :, at] = jnp.dot(
                heads[h], w_out[:, at], preferred_element_type=jnp.float32
            ).reshape(4, rb, cols)
            return carry

        lax.fori_loop(0, width // cols, chunk, 0)

    low_half = z < 2
    near = jnp.where(low_half, 1, -1)
    at_end = (z == 0) | (z == 3)

    def sum_hop(h, way, d):
        side = lax.div(way + 1, 2)
        return remote(
            rs_out.at[h, side, d],
            rs_in.at[h, side, d],
            rs_send.at[h, side, d],
            rs_recv.at[h, side, d],
            {"narrow": lax.rem(z + way + 4, 4)},
        )

    def near_target(i):
        return jnp.where(low_half, 3 - i, i)

    def sums_begin(h):
        @pl.when(at_end)
        def _():
            side = lax.div(near + 1, 2)
            for i in range(3):
                d = near_target(i)
                rs_out[h, side, d] = partial[h, d].astype(jnp.bfloat16)
                sum_hop(h, near, d).start()

    def sums_pass(h, way, d):
        @pl.when(jnp.logical_not(at_end))
        def _():
            side = lax.div(way + 1, 2)
            sum_hop(h, way, d).wait_recv()
            rs_out[h, side, d] = (partial[h, d] + rs_in[h, side, d].astype(jnp.float32)).astype(
                jnp.bfloat16
            )
            sum_hop(h, way, d).start()

    def sums_step(h, i):
        if i < 2:
            sums_pass(h, near, near_target(i))
        else:
            sums_pass(h, -near, near_target(3))

    def columns(k):
        return pl.ds(pl.multiple_of(lax.rem(z + k, 4) * cols, cols), cols)

    def finish_after(h):
        for way, there in ((1, z > 0), (-1, z < 3)):

            @pl.when(there)
            def _(way=way):
                side = (way + 1) // 2
                arrive(rs_in.at[h, side, z], rs_recv.at[h, side, z])
                partial[h, z] = partial[h, z] + rs_in[h, side, z].astype(jnp.float32)

        added = partial[h, z]
        own = pl.ds(pl.multiple_of(z * rb, rb), rb)
        tokens = jnp.concatenate([pieces[h, i, own, :] for i in range(4)], 1)
        rounded = (tokens.astype(jnp.float32) + added).astype(jnp.bfloat16)
        after[h] = rounded
        values = rounded.astype(jnp.float32)
        mean = jnp.mean(values * values, axis=1, keepdims=True)
        held[h, z, w] = (
            values * lax.rsqrt(mean + 1e-05) * gain_ref[1:2, :].astype(jnp.float32)
        ).astype(jnp.bfloat16)

    def after_push(h):
        for k in (1, 3, 2):
            push(
                after.at[h, :, columns(k)],
                after_in.at[h, k],
                after_send.at[h, k],
                after_recv.at[h, k],
                {"narrow": lax.rem(z + k, 4)},
            )

    def gate_columns():
        for r in range(1, 8):
            arrive(gates_in.at[r], gates_recv.at[r])
        gate_rows[...] = jnp.zeros_like(gate_rows)
        for r in range(8):
            for j in range(experts_held):
                at = r * experts_held + j
                gate_rows[at : at + 1, :] = jnp.sum(
                    jnp.where(expert == w * experts_held + j, gates_in[r], 0.0),
                    axis=0,
                    keepdims=True,
                )
        gate_cols[...] = gate_rows[...].T

    pushed = []

    def push_rows(slot, n, role, step):
        h, k = n // 4, n % 4
        ref = held.at[h, order[k], slot]
        push(ref, ref, send.at[len(pushed)], recv.at[role, n], {"wide": w + step})
        pushed.append(n)

    def arrive_rows(role, n):
        h, k = n // 4, n % 4
        arrive(held.at[h, order[k], slots[role]], recv.at[role, n])

    def along(h, src, way):
        return hop(held.at[h, src, w], z_send.at[h], z_recv.at[h], src, way)

    def pass_on(h, src):
        for way in (1, -1):

            @pl.when(sends(src, way))
            def _(way=way):
                along(h, src, way).start()

    def expert_rows(n):
        h, g = n // 4, order[n % 4]
        inputs = jnp.concatenate([held[h, g, slot] for slot in slots], 0)
        weights = gate_cols[pl.ds(pl.multiple_of(h * hr + g * rb, rb), rb), :]
        lanes = lax.broadcasted_iota(jnp.int32, weights.shape, 1)

        def one(j, carry):
            scale = jnp.concatenate(
                [
                    jnp.sum(
                        jnp.where(lanes == r * experts_held + j, weights, 0.0),
                        axis=1,
                        keepdims=True,
                    )
                    for r in range(8)
                ],
                0,
            )
            both = jnp.dot(inputs, gu[j], preferred_element_type=jnp.float32)
            gate = both[:, :inner]
            active = gate / (1.0 + jnp.exp(-gate)) * both[:, inner:] * scale
            weighted[h, :, g, :, pl.ds(pl.multiple_of(j * inner, inner), inner)] = active.astype(
                jnp.bfloat16
            ).reshape(8, rb, inner)
            return carry

        lax.fori_loop(0, experts_held, one, 0)

    turns = (2, 1, 3, 0)
    units = 4 * NH

    def product(m, low):
        h, k = m // 4, turns[m % 4]
        values = weighted[h, low : low + 4].reshape(4 * hr, experts_held * inner)
        return jnp.dot(
            values, down[:, columns(k)], preferred_element_type=jnp.float32
        ).reshape(4, hr, cols)

    sib_copies = {}

    def stage_sib(m):
        if m >= BUFFERS:
            sib_copies[m - BUFFERS].wait_send()
        sib_out[m % BUFFERS] = product(m, 4).astype(jnp.bfloat16)
        copy = remote(
            sib_out.at[m % BUFFERS], sib_in.at[m], r_send.at[m], r_recv.at[m], {"wide": w + sib}
        )
        copy.start()
        sib_copies[m] = copy

    def stage_first(m):
        value = product(m, 0)
        arrive(sib_in.at[m], r_recv.at[m])
        for spot, r in ((0, 1), (1, 3)):
            first_out[m, spot] = (value[r] + sib_in[m, r].astype(jnp.float32)).astype(jnp.bfloat16)
        at = units + m
        push(first_out.at[m], first_in.at[m], r_send.at[at], r_recv.at[at], {"wide": w + first})
        for spot, r in ((0, 0), (1, 2)):
            first_keep[m % 2, spot] = value[r] + sib_in[m, r].astype(jnp.float32)

    def stage_second(m):
        at = units + m
        arrive(first_in.at[m], r_recv.at[at])
        second_out[m] = (first_keep[m % 2, 1] + first_in[m, 1].astype(jnp.float32)).astype(
            jnp.bfloat16
        )
        at = 2 * units + m
        push(second_out.at[m], second_in.at[m], r_send.at[at], r_recv.at[at], {"wide": w + second})
        second_keep[m % 2] = first_keep[m % 2, 0] + first_in[m, 0].astype(jnp.float32)

    def stage_along(m):
        h, k = m // 4, turns[m % 4]
        at = 2 * units + m
        arrive(second_in.at[m], r_recv.at[at])
        value = second_keep[m % 2] + second_in[m].astype(jnp.float32)
        if k:
            z_out[m] = value.astype(jnp.bfloat16)
            at = 3 * units + m
            push(
                z_out.at[m],
                z_in.at[m],
                r_send.at[at],
                r_recv.at[at],
                {"narrow": lax.rem(z + k, 4)},
            )
        else:
            total[h] = value

    def finish(h):
        for k in (1, 2, 3):
            arrive(after_in.at[h, k], after_recv.at[h, k])
        for m in range(4 * h, 4 * h + 3):
            arrive(z_in.at[m], r_recv.at[3 * units + m])
            total[h] = total[h] + z_in[m].astype(jnp.float32)
        for k in range(4):
            group = lax.rem(z + 4 - k, 4)
            block = pl.ds(pl.multiple_of(group * rb, rb), rb)
            to = pl.ds(pl.multiple_of(h * hr + group * rb, rb), rb)
            own = after_in[h, k] if k else after[h, :, columns(0)]
            out_ref[to, :] = (total[h, block, :] + own.astype(jnp.float32)).astype(jnp.bfloat16)

    hidden_step(0, 1)
    part_chunk(0)
    part_chunk(1)
    hidden_step(0, 2)
    part_chunk(2)
    hidden_step(0, 3)
    hidden_pass(1, z)
    stats_push(0)
    part_chunk(3)
    contribute(1, z, True)
    stats_finish(0)
    load_cache.wait()
    attend(0, 0, EARLY_HEADS)
    hidden_step(1, 1)
    attend(0, EARLY_HEADS, count)
    load_out.wait()
    project(0)
    sums_begin(0)
    hidden_step(1, 2)
    sums_step(0, 0)
    hidden_step(1, 3)
    stats_push(1)
    sums_step(0, 1)
    sums_step(0, 2)
    gate_columns()
    stats_finish(1)
    attend(1, 0, EARLY_HEADS)
    finish_after(0)

    lead = 7
    for t in range(lead + units + 3):
        if t < units:
            h, k = t // 4, t % 4
            if h == 1 and k == 0:
                finish_after(1)
            if k == 0:
                pass_on(h, z)
            push_rows(w, t, 1, first)
            push_rows(w, t, 2, second)
            push_rows(w, t, 4, sib)
            if k == 0:
                after_push(h)
            if k < 3:
                src = order[k + 1]
                arrive(held.at[h, src, w], z_recv.at[h, src])
                pass_on(h, src)
        if 1 <= t < units + 1:
            n = t - 1
            arrive_rows(1, n)
            push_rows(slots[1], n, 3, second)
            push_rows(slots[1], n, 5, sib)
            arrive_rows(2, n)
            push_rows(slots[2], n, 6, sib)
        if 2 <= t < units + 2:
            n = t - 2
            arrive_rows(3, n)
            push_rows(slots[3], n, 7, sib)
        if t == 0:
            attend(1, EARLY_HEADS, count)
            project(1)
            sums_begin(1)
        if t == 1:
            sums_step(1, 0)
        if t == 2:
            sums_step(1, 1)
            sums_step(1, 2)
        if t == 3:
            load_down.wait()
        if lead <= t < lead + units:
            stage_sib(t - lead)
        if lead + 1 <= t < lead + units + 1:
            stage_first(t - lead - 1)
        if 3 <= t < units + 3:
            n = t - 3
            for role in (4, 5, 6, 7):
                arrive_rows(role, n)
            expert_rows(n)
        if lead + 2 <= t < lead + units + 2:
            stage_second(t - lead - 2)
        if lead + 3 <= t:
            stage_along(t - lead - 3)
        if t == lead + 8:
            finish(0)
    finish(1)
    for copy in started:
        copy.wait_send()
    for m in range(units - BUFFERS, units):
        sib_copies[m].wait_send()
    for h in range(NH):
        for src in order:
            for way in (1, -1):

                @pl.when(sends(src, way))
                def _(h=h, src=src, way=way):
                    hidden_hop(h, src, way).wait_send()
                    along(h, src, way).wait_send()

        @pl.when(at_end)
        def _(h=h):
            for i in range(3):
                sum_hop(h, near, near_target(i)).wait_send()

        @pl.when(jnp.logical_not(at_end))
        def _(h=h):
            for i in range(2):
                sum_hop(h, near, near_target(i)).wait_send()
            sum_hop(h, -near, near_target(3)).wait_send()


def layer_by_copies(
    hidden, norm_gain, w_qkv, qk_gain, w_out, cache, lengths, placing, routes, gate_w, w_gu, w_down
):
    _, span, cols = hidden.shape
    width = cols * 4
    held, _, _, inner = w_gu.shape
    experts = held * 8
    hr, rb = span // NH, span // NH // 4
    units = 4 * NH
    half, full = jnp.bfloat16, jnp.float32
    vmem = pl.BlockSpec(memory_space=pltpu.VMEM)
    smem = pl.BlockSpec(memory_space=pltpu.SMEM)
    anywhere = pl.BlockSpec(memory_space=pl.ANY)
    dma = pltpu.SemaphoreType.DMA
    scratch = pltpu.VMEM
    result, fresh = pl.pallas_call(
        layer_kernel,
        out_shape=(
            jax.ShapeDtypeStruct((span, cols), half),
            jax.ShapeDtypeStruct((2, span, cols), half),
        ),
        in_specs=[smem] * 2 + [vmem] * 5 + [anywhere] * 5,
        out_specs=(vmem, vmem),
        scratch_shapes=[
            scratch((NH, 4, hr, cols), half),
            scratch((3, width, cols), half),
            scratch((2,) + cache.shape[2:], half),
            scratch(w_out.shape, half),
            scratch((2, RAW_ROWS, 2, inner), half),
            scratch((held, width, 2 * inner), half),
            scratch((held * inner, width), half),
            scratch((2, span, HD), full),
            scratch((8, experts, span), full),
            scratch((128, span), full),
            scratch((span, 128), full),
            scratch((NH, 3, hr, cols), full),
            scratch((NH, hr, 128), full),
            scratch((NH, hr, cols), half),
            scratch((NH, 8, hr), full),
            scratch((NH, 4, 8, hr), full),
            scratch((NH, 4, rb, width), full),
            scratch((NH, 2, 4, rb, width), half),
            scratch((NH, 2, 4, rb, width), half),
            scratch((NH, rb, width), half),
            scratch((NH, 4, rb, cols), half),
            scratch((NH, 4, 8, rb, width), half),
            scratch((NH, 8, 4, rb, held * inner), half),
            scratch((BUFFERS, 4, hr, cols), half),
            scratch((units, 4, hr, cols), half),
            scratch((units, 2, hr, cols), half),
            scratch((2, 2, hr, cols), full),
            scratch((units, 2, hr, cols), half),
            scratch((units, hr, cols), half),
            scratch((2, hr, cols), full),
            scratch((units, hr, cols), half),
            scratch((units, hr, cols), half),
            scratch((units, hr, cols), half),
            scratch((NH, hr, cols), full),
            dma((4,)),
            dma((2,)),
            dma((NH, 2, 4)),
            dma((NH, 4)),
            dma((8,)),
            dma((8,)),
            dma((NH, 4)),
            dma((NH, 4)),
            dma((NH, 2, 4)),
            dma((NH, 2, 4)),
            dma((NH, 4)),
            dma((NH, 4)),
            dma((7 * units,)),
            dma((8, units)),
            dma((NH, 2, 4)),
            dma((NH, 4)),
            dma((4 * units,)),
            dma((4 * units,)),
        ],
        compiler_params=pltpu.CompilerParams(
            collective_id=0, has_side_effects=True, vmem_limit_bytes=VMEM_LIMIT
        ),
        name="layer",
    )(
        lengths,
        placing,
        hidden[0],
        norm_gain,
        qk_gain,
        jnp.transpose(routes[0]),
        jnp.transpose(gate_w[0]),
        jnp.transpose(w_qkv, (1, 0, 2)),
        cache[:, 0],
        w_out,
        w_gu,
        w_down.reshape(held * inner, width),
    )
    return result[None], fresh[:, None]


def router_table(routes, gate_w, experts):
    named = routes[:, :, None] == jnp.arange(experts, dtype=jnp.int32)[None, None, :]
    return jnp.sum(jnp.where(named, gate_w[:, :, None], 0.0), axis=1)


def experts_by_collectives(after_rows, gain, routes, gate_w, w_gu, w_down):
    position = lax.axis_index("wide")
    column = lax.axis_index("narrow")
    wide_size = lax.axis_size("wide")
    narrow = lax.axis_size("narrow")
    rows, full_width = after_rows.shape
    span_len, share_cols = rows * narrow, full_width // narrow
    after_all = lax.all_gather(after_rows, ("wide", "narrow"), axis=0, tiled=True)
    after_own = lax.dynamic_slice(
        after_all, (position * span_len, column * share_cols), (span_len, share_cols)
    )
    routed = normalize(after_all, gain).astype(jnp.bfloat16)
    held_experts = w_gu.shape[0]
    inner_cols = w_gu.shape[3]
    experts = held_experts * wide_size
    table = router_table(routes, gate_w, experts)
    table = lax.all_gather(table, "wide", axis=0, tiled=True)
    scale = lax.dynamic_slice_in_dim(table, position * held_experts, held_experts, 1)
    pieces = []
    for j in range(held_experts):
        gate_up = jnp.dot(
            routed,
            w_gu[j].reshape(full_width, 2 * inner_cols),
            preferred_element_type=jnp.float32,
        )
        activated = jax.nn.silu(gate_up[:, :inner_cols]) * gate_up[:, inner_cols:]
        pieces.append((activated * scale[:, j : j + 1]).astype(jnp.bfloat16))
    weighted = jnp.concatenate(pieces, 1)
    combined = jnp.dot(
        weighted,
        w_down.reshape(held_experts * inner_cols, full_width),
        preferred_element_type=jnp.float32,
    ).astype(jnp.bfloat16)
    combined = lax.psum_scatter(combined, "wide", scatter_dimension=0, tiled=True)
    expert_out = lax.psum_scatter(
        combined, "narrow", scatter_dimension=1, tiled=True
    ).astype(jnp.float32)
    return (after_own.astype(jnp.float32) + expert_out).astype(jnp.bfloat16)

def per_device(
    hidden, norm_gain, w_qkv, qk_gain, w_out, cache, lengths, placing, routes, gate_w, w_gu, w_down
):
    narrow = lax.axis_size("narrow")
    column = lax.axis_index("narrow")
    position = lax.axis_index("wide")
    span_len = hidden.shape[1]
    share_cols = hidden.shape[2]
    full_width = share_cols * narrow
    tokens = lax.all_gather(hidden[0], "narrow", axis=1, tiled=True)
    normed = normalize(tokens, norm_gain[0]).astype(jnp.bfloat16)
    local_cols = w_qkv.shape[2]
    projected = jnp.dot(
        normed, w_qkv.reshape(full_width, 3 * local_cols), preferred_element_type=jnp.float32
    )
    queries = projected[:, :local_cols]
    keys_new = projected[:, local_cols : 2 * local_cols]
    values_new = projected[:, 2 * local_cols :]
    squares = lax.psum((jnp.sum(queries * queries, -1), jnp.sum(keys_new * keys_new, -1)), "narrow")
    features = local_cols * narrow
    queries = queries * lax.rsqrt(squares[0][:, None] / features + 1e-05) * qk_gain[0]
    keys_new = keys_new * lax.rsqrt(squares[1][:, None] / features + 1e-05) * qk_gain[1]
    head_count = local_cols // HD
    length = lengths[placing[position]]
    positions = length.astype(jnp.float32) + jnp.arange(span_len, dtype=jnp.float32)
    queries = rotary(queries.reshape(span_len, head_count, HD), positions).astype(jnp.bfloat16)
    keys_new = rotary(keys_new.reshape(span_len, head_count, HD), positions).astype(jnp.bfloat16)
    values_new = values_new.reshape(span_len, head_count, HD).astype(jnp.bfloat16)
    stored = cache.shape[2]
    all_keys = jnp.concatenate([cache[0, 0].reshape(stored, head_count, HD), keys_new], 0)
    all_values = jnp.concatenate([cache[1, 0].reshape(stored, head_count, HD), values_new], 0)
    scores = jnp.einsum(
        "thd,jhd->htj", queries, all_keys, preferred_element_type=jnp.float32
    ) * HD ** (-0.5)
    key_index = jnp.arange(stored + span_len, dtype=jnp.int32)[None, :]
    query_index = jnp.arange(span_len, dtype=jnp.int32)[:, None]
    allowed = jnp.where(key_index < stored, key_index < length, key_index - stored <= query_index)
    scores = jnp.where(allowed[None], scores, -1e30)
    highest = jnp.max(scores, axis=-1, keepdims=True)
    exponent = jnp.exp(scores - highest)
    weights = exponent.astype(jnp.bfloat16)
    denominator = jnp.sum(exponent, axis=-1)
    summed = jnp.einsum("htj,jhd->thd", weights, all_values, preferred_element_type=jnp.float32)
    heads_out = (
        (summed / jnp.transpose(denominator)[:, :, None])
        .astype(jnp.bfloat16)
        .reshape(span_len, local_cols)
    )
    partial_out = jnp.dot(heads_out, w_out, preferred_element_type=jnp.float32)
    rows = span_len // narrow
    attention = lax.psum_scatter(
        partial_out.astype(jnp.bfloat16), "narrow", scatter_dimension=0, tiled=True
    ).astype(jnp.float32)
    own_rows = lax.dynamic_slice_in_dim(tokens, column * rows, rows, 0)
    after_rows = (own_rows.astype(jnp.float32) + attention).astype(jnp.bfloat16)
    result = experts_by_collectives(
        after_rows, norm_gain[1], routes[0], gate_w[0], w_gu, w_down
    )[None]
    fresh = jnp.stack(
        [keys_new.reshape(span_len, local_cols), values_new.reshape(span_len, local_cols)]
    )[:, None]
    return (result, fresh)


def solution(mesh):
    placed = (
        P("wide", None, "narrow"),
        P(),
        P(None, None, "narrow"),
        P(None, "narrow"),
        P("narrow", None),
        P(None, "wide", None, "narrow"),
        P(),
        P(),
        P("wide", None, None),
        P("wide", None, None),
        P("wide", None, None, "narrow"),
        P("wide", "narrow", None),
    )
    by_copies = mesh.shape["wide"] == 8 and mesh.shape["narrow"] == 4
    return jax.shard_map(
        layer_by_copies if by_copies else per_device,
        mesh=mesh,
        in_specs=placed,
        out_specs=(P("wide", None, "narrow"), P(None, "wide", None, "narrow")),
        check_vma=False,
    )
```

```python
import math

import jax
import jax.numpy as jnp
from jax import lax
from jax.experimental import pallas as pl
from jax.experimental.pallas import tpu as pltpu
from jax.sharding import PartitionSpec as P

HD = 128


def normalize(values, gain_row):
    values = values.astype(jnp.float32)
    return (
        values
        * lax.rsqrt(jnp.mean(values * values, axis=-1, keepdims=True) + 1e-05)
        * gain_row.astype(jnp.float32)
    )


def rotary(values, positions):
    half_dim = values.shape[-1] // 2
    frequency = 10000.0 ** (-(jnp.arange(half_dim, dtype=jnp.float32) * (2.0 / values.shape[-1])))
    angle = positions[:, None] * frequency[None, :]
    cosine = jnp.cos(angle)[:, None, :]
    sine_part = jnp.sin(angle)[:, None, :]
    first_half = values[..., :half_dim]
    second_half = values[..., half_dim:]
    return jnp.concatenate(
        [
            first_half * cosine - second_half * sine_part,
            second_half * cosine + first_half * sine_part,
        ],
        axis=-1,
    )


NH = 2
BUFFERS = 4
RAW_ROWS = 1024
VMEM_LIMIT = 60 * 1024 * 1024
INVERSE = (0, 1, 2, 3, 4, 6, 5, 7)
EARLY_HEADS = 2
G_AT = (0, 1, 3, 4)
R_AT = (0, 1, 2, 3)
SUMS_AT = (0, 1, 2, 4)
KEEP = 2
TAIL_CUTS = 1
AFTER_AT = 13


def places():
    w = lax.axis_index("wide")
    z = lax.axis_index("narrow")
    c = lax.rem(w, 2)
    dx = 2 - 4 * lax.rem(lax.div(w, 2), 2)
    dy = 4 - 8 * lax.div(w, 4)
    first = dx * (1 - c) + dy * c
    second = dy * (1 - c) + dx * c
    return w, z, 1 - 2 * c, first, second


def layer_kernel(
    lengths_ref,
    placing_ref,
    hidden_ref,
    gain_ref,
    qk_gain_ref,
    routes_ref,
    gate_ref,
    w_qkv_any,
    cache_any,
    w_out_any,
    gu_any,
    down_any,
    out_ref,
    fresh_ref,
    pieces,
    w_qkv,
    cache,
    w_out,
    raw,
    gu,
    down,
    rope,
    gates_in,
    gate_rows,
    gate_cols,
    projected,
    squares,
    heads,
    stat_out,
    stat_in,
    partial,
    rs_out,
    rs_in,
    after,
    after_in,
    held,
    weighted,
    sib_out,
    sib_in,
    first_out,
    first_keep,
    first_in,
    second_out,
    second_keep,
    second_in,
    z_out,
    z_in,
    total,
    loads,
    raw_loads,
    h_send,
    h_recv,
    gates_send,
    gates_recv,
    stat_send,
    stat_recv,
    rs_send,
    rs_recv,
    after_send,
    after_recv,
    send,
    recv,
    z_send,
    z_recv,
    r_send,
    r_recv,
):
    w, z, sib, first, second = places()
    span, cols = hidden_ref.shape
    width = cols * 4
    hr = span // NH
    rb = hr // 4
    inner = gu.shape[2] // 2
    experts_held = gu.shape[0]
    steps = (
        0,
        first,
        second,
        first + second,
        sib,
        sib + second,
        sib + first,
        sib + first + second,
    )
    slots = [w + step for step in steps]
    upper = lax.div(z, 2)
    order = (z, z + 1 - 2 * lax.rem(z, 2), 2 - upper, 3 - 3 * upper)
    started = []

    def remote(src, dst, send_sem, recv_sem, device):
        return pltpu.make_async_remote_copy(
            src_ref=src,
            dst_ref=dst,
            send_sem=send_sem,
            recv_sem=recv_sem,
            device_id=device,
            device_id_type=pl.DeviceIdType.MESH,
        )

    def push(src, dst, send_sem, recv_sem, device):
        copy = remote(src, dst, send_sem, recv_sem, device)
        copy.start()
        started.append(copy)
        return copy

    def arrive(dst, recv_sem):
        remote(dst, dst, r_send.at[0], recv_sem, {"wide": w + sib}).wait_recv()

    load_qkv = pltpu.make_async_copy(w_qkv_any, w_qkv, loads.at[0])
    load_cache = pltpu.make_async_copy(cache_any, cache, loads.at[1])
    load_out = pltpu.make_async_copy(w_out_any, w_out, loads.at[2])
    load_down = pltpu.make_async_copy(down_any, down, loads.at[3])
    per_expert = width // RAW_ROWS
    chunks = experts_held * per_expert

    def load_raw(i):
        e, part = i // per_expert, i % per_expert
        return pltpu.make_async_copy(
            gu_any.at[e, pl.ds(part * RAW_ROWS, RAW_ROWS)], raw.at[i % 2], raw_loads.at[i % 2]
        )

    load_qkv.start()
    load_raw(0).start()
    load_raw(1).start()

    barrier = pltpu.get_barrier_semaphore()
    for step in steps[1:]:
        pl.semaphore_signal(
            barrier, inc=1, device_id={"wide": w + step}, device_id_type=pl.DeviceIdType.MESH
        )
    for k in (1, 2, 3):
        pl.semaphore_signal(
            barrier, inc=1, device_id={"narrow": order[k]}, device_id_type=pl.DeviceIdType.MESH
        )
    for h in range(NH):
        pieces[h, z] = hidden_ref[h * hr : (h + 1) * hr]
    pl.semaphore_wait(barrier, 10)

    def hop(buffer, send_sems, recv_sems, src, way):
        return remote(
            buffer,
            buffer,
            send_sems.at[(way + 1) // 2, src],
            recv_sems.at[src],
            {"narrow": lax.rem(z + way + 4, 4)},
        )

    def sends(src, way):
        if way > 0:
            return (src <= z) & (z < 3) & jnp.logical_not((src == 0) & (z == 2))
        return (src >= z) & (z > 0) & jnp.logical_not((src == 3) & (z == 1))

    low_half = z < 2
    near = jnp.where(low_half, 1, -1)
    at_end = (z == 0) | (z == 3)
    across_side = lax.div(1 - near, 2)

    def across_hop(buffer, send_sems, recv_sems):
        return remote(
            buffer, buffer, send_sems.at[across_side, z], recv_sems.at[z], {"narrow": 3 - z}
        )

    def hidden_hop(h, src, way):
        return hop(pieces.at[h, src], h_send.at[h], h_recv.at[h], src, way)

    def hidden_pass(h, src):
        for way in (1, -1):

            @pl.when(sends(src, way))
            def _(way=way):
                hidden_hop(h, src, way).start()

    def hidden_begin(h):
        @pl.when(at_end)
        def _():
            across_hop(pieces.at[h, z], h_send.at[h], h_recv.at[h]).start()

        hidden_pass(h, z)

    hidden_begin(0)
    load_cache.start()
    load_out.start()
    load_down.start()

    expert = lax.broadcasted_iota(jnp.int32, gates_in.shape[1:], 0)
    table = jnp.zeros(gates_in.shape[1:], jnp.float32)
    for k in range(routes_ref.shape[0]):
        table = table + jnp.where(routes_ref[k : k + 1, :] == expert, gate_ref[k : k + 1, :], 0.0)
    gates_in[0] = table
    for r in range(1, 8):
        push(
            gates_in.at[0],
            gates_in.at[INVERSE[r]],
            gates_send.at[r],
            gates_recv.at[INVERSE[r]],
            {"wide": w + steps[r]},
        )

    length = lengths_ref[placing_ref[w]]
    lane = lax.broadcasted_iota(jnp.int32, (1, HD), 1)
    frequency = jnp.exp(
        lax.rem(lane, HD // 2).astype(jnp.float32) * (-2.0 / HD * math.log(10000.0))
    )
    positions = (length + lax.broadcasted_iota(jnp.int32, (span, 1), 0)).astype(jnp.float32)
    angle = positions * frequency
    rope[0] = jnp.cos(angle)
    rope[1] = jnp.sin(angle) * jnp.where(lane < HD // 2, -1.0, 1.0)

    def contribute(h, src, start):
        values = pieces[h, src].astype(jnp.float32)
        at = pl.ds(pl.multiple_of(src * cols, cols), cols)
        scaled = (values * gain_ref[0:1, at].astype(jnp.float32)).astype(jnp.bfloat16)
        square = jnp.sum(values * values, axis=1, keepdims=True)
        for i in range(3):
            term = jnp.dot(scaled, w_qkv[i, at, :], preferred_element_type=jnp.float32)
            projected[h, i] = term if start else projected[h, i] + term
        wide = jnp.broadcast_to(square, squares.shape[1:])
        squares[h] = wide if start else squares[h] + wide

    def hidden_step(h, k):
        arrive(pieces.at[h, order[k]], h_recv.at[h, order[k]])
        hidden_pass(h, order[k])
        contribute(h, order[k], False)

    load_qkv.wait()
    contribute(0, z, True)

    row = lax.broadcasted_iota(jnp.int32, (256, 256), 0)
    column = lax.broadcasted_iota(jnp.int32, (256, 256), 1)
    part_them = (column == jnp.where(row < 128, 2 * row, 2 * row - 255)).astype(jnp.bfloat16)

    def part_chunk(i):
        load_raw(i).wait()

        def part(n, carry):
            at = pl.ds(pl.multiple_of(n * 128, 128), 128)
            to = pl.ds(pl.multiple_of(i % per_expert * RAW_ROWS + n * 128, 128), 128)
            both = jnp.dot(
                part_them,
                raw[i % 2, at].reshape(256, inner),
                preferred_element_type=jnp.float32,
            ).astype(jnp.bfloat16)
            gu[i // per_expert, to, 0:inner] = both[:128]
            gu[i // per_expert, to, inner : 2 * inner] = both[128:]
            return carry

        lax.fori_loop(0, RAW_ROWS // 128, part, 0)
        if i + 2 < chunks:
            load_raw(i + 2).start()

    def stats_push(h):
        scale = lax.rsqrt(squares[h, :, :1] / width + 1e-05)
        for i in range(3):
            projected[h, i] = projected[h, i] * scale
        spot = lax.broadcasted_iota(jnp.int32, (hr, 128), 1)
        both = [
            jnp.sum(projected[h, i] * projected[h, i], axis=1, keepdims=True) for i in range(2)
        ]
        sums = jnp.where(spot == 0, both[0], jnp.where(spot == 1, both[1], 0.0))
        stat_out[h] = sums.T[:8]
        for k in (1, 2, 3):
            push(
                stat_out.at[h],
                stat_in.at[h, z],
                stat_send.at[h, k],
                stat_recv.at[h, z],
                {"narrow": order[k]},
            )
        fresh_ref[1, h * hr : (h + 1) * hr] = projected[h, 2].astype(jnp.bfloat16)

    def stats_finish(h):
        totals = stat_out[h]
        for k in (1, 2, 3):
            arrive(stat_in.at[h, order[k]], stat_recv.at[h, order[k]])
            totals = totals + stat_in[h, order[k]]
        turned = jnp.concatenate([totals, jnp.zeros((120, hr), jnp.float32)], 0).T
        scales = lax.rsqrt(turned / width + 1e-05)
        for i in range(2):
            projected[h, i] = projected[h, i] * scales[:, i : i + 1] * qk_gain_ref[i : i + 1, :]

    across = (((1,), (1,)), ((), ()))
    stored = cache.shape[1]
    exponent_scale = HD ** (-0.5) * math.log2(math.e)

    def attend(h, low, high):
        rows = slice(h * hr, (h + 1) * hr)
        seen = (h + 1) * hr
        old_allowed = lax.broadcasted_iota(jnp.int32, (1, stored), 1) < length
        new_allowed = lax.broadcasted_iota(jnp.int32, (hr, seen), 1) <= h * hr + (
            lax.broadcasted_iota(jnp.int32, (hr, seen), 0)
        )

        def head(n, carry):
            at = pl.ds(pl.multiple_of(n * HD, HD), HD)
            cosine, sine = rope[0, rows], rope[1, rows]

            def turned(i):
                values = projected[h, i, :, at]
                return (values * cosine + pltpu.roll(values, HD // 2, 1) * sine).astype(
                    jnp.bfloat16
                )

            query = turned(0)
            fresh_ref[0, rows, at] = turned(1)
            old = lax.dot_general(
                query, cache[0, :, at], across, preferred_element_type=jnp.float32
            )
            new = lax.dot_general(
                query, fresh_ref[0, :seen, at], across, preferred_element_type=jnp.float32
            )
            old = jnp.where(old_allowed, old, -1e30)
            new = jnp.where(new_allowed, new, -1e30)
            highest = jnp.maximum(
                jnp.max(old, axis=1, keepdims=True), jnp.max(new, axis=1, keepdims=True)
            )
            old = jnp.exp2((old - highest) * exponent_scale)
            new = jnp.exp2((new - highest) * exponent_scale)
            denominator = jnp.sum(old, axis=1, keepdims=True) + jnp.sum(
                new, axis=1, keepdims=True
            )
            summed = jnp.dot(
                old.astype(jnp.bfloat16), cache[1, :, at], preferred_element_type=jnp.float32
            ) + jnp.dot(
                new.astype(jnp.bfloat16),
                fresh_ref[1, :seen, at],
                preferred_element_type=jnp.float32,
            )
            heads[h, :, at] = (summed / denominator).astype(jnp.bfloat16)
            return carry

        lax.fori_loop(low, high, head, 0)

    count = cols // HD

    def project(h):
        def chunk(i, carry):
            at = pl.ds(pl.multiple_of(i * cols, cols), cols)
            partial[h, :, :, at] = jnp.dot(
                heads[h], w_out[:, at], preferred_element_type=jnp.float32
            ).reshape(4, rb, cols)
            return carry

        lax.fori_loop(0, width // cols, chunk, 0)

    def sum_hop(h, way, d):
        side = lax.div(way + 1, 2)
        return remote(
            rs_out.at[h, side, d],
            rs_in.at[h, side, d],
            rs_send.at[h, side, d],
            rs_recv.at[h, side, d],
            {"narrow": lax.rem(z + way + 4, 4)},
        )

    def sum_across(h):
        return remote(
            rs_out.at[h, across_side, 3 - z],
            rs_in.at[h, across_side, 3 - z],
            rs_send.at[h, across_side, 3 - z],
            rs_recv.at[h, across_side, 3 - z],
            {"narrow": 3 - z},
        )

    def near_target(i):
        return jnp.where(low_half, 3 - i, i)

    def sums_begin(h):
        d = near_target(0)
        side = jnp.where(at_end, across_side, lax.div(near + 1, 2))
        rs_out[h, side, d] = partial[h, d].astype(jnp.bfloat16)

        @pl.when(at_end)
        def _():
            sum_across(h).start()
            for i in (1, 2):
                to = near_target(i)
                rs_out[h, lax.div(near + 1, 2), to] = partial[h, to].astype(jnp.bfloat16)
                sum_hop(h, near, to).start()

        @pl.when(jnp.logical_not(at_end))
        def _():
            sum_hop(h, near, d).start()

    def sums_pass(h, way, d):
        @pl.when(jnp.logical_not(at_end))
        def _():
            side = lax.div(way + 1, 2)
            sum_hop(h, way, d).wait_recv()
            rs_out[h, side, d] = (partial[h, d] + rs_in[h, side, d].astype(jnp.float32)).astype(
                jnp.bfloat16
            )
            sum_hop(h, way, d).start()

    def sums_step(h, i):
        if i == 0:
            sums_pass(h, near, near_target(1))
        else:
            sums_pass(h, -near, near_target(3))

    def columns(k):
        return pl.ds(pl.multiple_of(lax.rem(z + k, 4) * cols, cols), cols)

    def finish_after(h):
        for side in range(2):
            arrive(rs_in.at[h, side, z], rs_recv.at[h, side, z])
        added = (
            partial[h, z]
            + rs_in[h, 0, z].astype(jnp.float32)
            + rs_in[h, 1, z].astype(jnp.float32)
        )
        own = pl.ds(pl.multiple_of(z * rb, rb), rb)
        tokens = jnp.concatenate([pieces[h, i, own, :] for i in range(4)], 1)
        rounded = (tokens.astype(jnp.float32) + added).astype(jnp.bfloat16)
        after[h] = rounded
        values = rounded.astype(jnp.float32)
        mean = jnp.mean(values * values, axis=1, keepdims=True)
        held[h, z, w] = (
            values * lax.rsqrt(mean + 1e-05) * gain_ref[1:2, :].astype(jnp.float32)
        ).astype(jnp.bfloat16)

    def after_push(h):
        for k in (1, 3, 2):
            push(
                after.at[h, :, columns(k)],
                after_in.at[h, k],
                after_send.at[h, k],
                after_recv.at[h, k],
                {"narrow": lax.rem(z + k, 4)},
            )

    def gate_columns():
        for r in range(1, 8):
            arrive(gates_in.at[r], gates_recv.at[r])
        gate_rows[...] = jnp.zeros_like(gate_rows)
        for r in range(8):
            for j in range(experts_held):
                at = r * experts_held + j
                gate_rows[at : at + 1, :] = jnp.sum(
                    jnp.where(expert == w * experts_held + j, gates_in[r], 0.0),
                    axis=0,
                    keepdims=True,
                )
        gate_cols[...] = gate_rows[...].T

    pushed = []

    def push_rows(slot, n, role, step):
        h, k = n // 4, n % 4
        ref = held.at[h, order[k], slot]
        push(ref, ref, send.at[len(pushed)], recv.at[role, n], {"wide": w + step})
        pushed.append(n)

    def arrive_rows(role, n):
        h, k = n // 4, n % 4
        arrive(held.at[h, order[k], slots[role]], recv.at[role, n])

    def along(h, src, way):
        return hop(held.at[h, src, w], z_send.at[h], z_recv.at[h], src, way)

    def pass_on(h, k):
        src = order[k]
        if k == 0:

            @pl.when(at_end)
            def _():
                across_hop(held.at[h, z, w], z_send.at[h], z_recv.at[h]).start()

        for way in (1, -1):

            @pl.when(sends(src, way))
            def _(way=way):
                along(h, src, way).start()

    def expert_rows(n):
        h, g = n // 4, order[n % 4]
        inputs = jnp.concatenate([held[h, g, slot] for slot in slots], 0)
        weights = gate_cols[pl.ds(pl.multiple_of(h * hr + g * rb, rb), rb), :]
        lanes = lax.broadcasted_iota(jnp.int32, weights.shape, 1)

        def one(j, carry):
            scale = jnp.concatenate(
                [
                    jnp.sum(
                        jnp.where(lanes == r * experts_held + j, weights, 0.0),
                        axis=1,
                        keepdims=True,
                    )
                    for r in range(8)
                ],
                0,
            )
            both = jnp.dot(inputs, gu[j], preferred_element_type=jnp.float32)
            gate = both[:, :inner]
            active = gate / (1.0 + jnp.exp(-gate)) * both[:, inner:] * scale
            weighted[h, :, g, :, pl.ds(pl.multiple_of(j * inner, inner), inner)] = active.astype(
                jnp.bfloat16
            ).reshape(8, rb, inner)
            return carry

        lax.fori_loop(0, experts_held, one, 0)

    turns = (2, 1, 3, 0)
    units = 4 * NH

    cuts = [(m, 0, cols) for m in range(units - 1)] + [
        (units - 1, c * (cols // TAIL_CUTS), cols // TAIL_CUTS) for c in range(TAIL_CUTS)
    ]
    parts = len(cuts)

    def product(u, low):
        m, start, size = cuts[u]
        h, k = m // 4, turns[m % 4]
        values = weighted[h, low : low + 4].reshape(4 * hr, experts_held * inner)
        at = pl.ds(pl.multiple_of(lax.rem(z + k, 4) * cols + start, size), size)
        return jnp.dot(values, down[:, at], preferred_element_type=jnp.float32).reshape(
            4, hr, size
        )

    sib_copies = {}

    def spot_of(u):
        m, start, size = cuts[u]
        return m, slice(start, start + size), pl.ds(start, size)

    def stage_sib(u):
        m, at, to = spot_of(u)
        if m >= BUFFERS and cuts[u][1] == 0:
            sib_copies[m - BUFFERS].wait_send()
        sib_out[m % BUFFERS, :, :, at] = product(u, 4).astype(jnp.bfloat16)
        copy = remote(
            sib_out.at[m % BUFFERS, :, :, to],
            sib_in.at[m, :, :, to],
            r_send.at[u],
            r_recv.at[u],
            {"wide": w + sib},
        )
        copy.start()
        sib_copies[u] = copy

    def stage_first(u):
        m, at, to = spot_of(u)
        value = product(u, 0)
        arrive(sib_in.at[m, :, :, to], r_recv.at[u])
        for spot, r in ((0, 1), (1, 3)):
            first_out[m, spot, :, at] = (
                value[r] + sib_in[m, r, :, at].astype(jnp.float32)
            ).astype(jnp.bfloat16)
        push(
            first_out.at[m, :, :, to],
            first_in.at[m, :, :, to],
            r_send.at[parts + u],
            r_recv.at[parts + u],
            {"wide": w + first},
        )
        for spot, r in ((0, 0), (1, 2)):
            first_keep[m % KEEP, spot, :, at] = value[r] + sib_in[m, r, :, at].astype(jnp.float32)

    def stage_second(u):
        m, at, to = spot_of(u)
        arrive(first_in.at[m, :, :, to], r_recv.at[parts + u])
        second_out[m, :, at] = (
            first_keep[m % KEEP, 1, :, at] + first_in[m, 1, :, at].astype(jnp.float32)
        ).astype(jnp.bfloat16)
        push(
            second_out.at[m, :, to],
            second_in.at[m, :, to],
            r_send.at[2 * parts + u],
            r_recv.at[2 * parts + u],
            {"wide": w + second},
        )
        second_keep[m % KEEP, :, at] = first_keep[m % KEEP, 0, :, at] + first_in[
            m, 0, :, at
        ].astype(jnp.float32)

    def stage_along(u):
        m, at, to = spot_of(u)
        h, k = m // 4, turns[m % 4]
        arrive(second_in.at[m, :, to], r_recv.at[2 * parts + u])
        value = second_keep[m % KEEP, :, at] + second_in[m, :, at].astype(jnp.float32)
        if k:
            z_out[m] = value.astype(jnp.bfloat16)
            push(
                z_out.at[m],
                z_in.at[m],
                r_send.at[3 * parts + m],
                r_recv.at[3 * parts + m],
                {"narrow": lax.rem(z + k, 4)},
            )
        else:
            total[h, :, at] = value

    def finish(h):
        for k in (1, 2, 3):
            arrive(after_in.at[h, k], after_recv.at[h, k])
        for m in range(4 * h, 4 * h + 3):
            arrive(z_in.at[m], r_recv.at[3 * parts + m])
            total[h] = total[h] + z_in[m].astype(jnp.float32)
        for k in range(4):
            group = lax.rem(z + 4 - k, 4)
            block = pl.ds(pl.multiple_of(group * rb, rb), rb)
            to = pl.ds(pl.multiple_of(h * hr + group * rb, rb), rb)
            own = after_in[h, k] if k else after[h, :, columns(0)]
            out_ref[to, :] = (total[h, block, :] + own.astype(jnp.float32)).astype(jnp.bfloat16)

    part_chunk(0)
    hidden_step(0, 1)
    hidden_step(0, 2)
    part_chunk(1)
    hidden_step(0, 3)
    stats_push(0)
    hidden_begin(1)
    contribute(1, z, True)
    stats_finish(0)
    load_cache.wait()
    attend(0, 0, EARLY_HEADS)
    hidden_step(1, 1)
    attend(0, EARLY_HEADS, count)
    load_out.wait()
    project(0)
    sums_begin(0)
    hidden_step(1, 2)
    sums_step(0, 0)
    hidden_step(1, 3)
    stats_push(1)
    sums_step(0, 1)
    gate_columns()
    stats_finish(1)
    attend(1, 0, EARLY_HEADS)
    finish_after(0)

    lead = 4 + G_AT[3]
    for t in range(lead + parts + R_AT[3]):
        if t == SUMS_AT[3]:
            finish_after(1)
        if t < units:
            h, k = t // 4, t % 4
            if k == 0:
                pass_on(h, 0)
            push_rows(w, t, 1, first)
            push_rows(w, t, 2, second)
            push_rows(w, t, 4, sib)
            if k < 3:
                src = order[k + 1]
                arrive(held.at[h, src, w], z_recv.at[h, src])
                pass_on(h, k + 1)
        n = t - G_AT[1]
        if 0 <= n < units:
            arrive_rows(1, n)
            push_rows(slots[1], n, 3, second)
            push_rows(slots[1], n, 5, sib)
            arrive_rows(2, n)
            push_rows(slots[2], n, 6, sib)
        n = t - G_AT[2]
        if 0 <= n < units:
            arrive_rows(3, n)
            push_rows(slots[3], n, 7, sib)
        if t == SUMS_AT[0]:
            attend(1, EARLY_HEADS, count)
            project(1)
            sums_begin(1)
        for i in range(2):
            if t == SUMS_AT[1 + i]:
                sums_step(1, i)
        if t == 3:
            load_down.wait()
        if t in (1, 2):
            part_chunk(t + 1)
        if t == AFTER_AT:
            after_push(0)
            after_push(1)
        m = t - lead
        if 0 <= m - R_AT[0] < parts:
            stage_sib(m - R_AT[0])
        if 0 <= m - R_AT[1] < parts:
            stage_first(m - R_AT[1])
        n = t - G_AT[3]
        if 0 <= n < units:
            for role in (4, 5, 6, 7):
                arrive_rows(role, n)
            expert_rows(n)
        if 0 <= m - R_AT[2] < parts:
            stage_second(m - R_AT[2])
        if 0 <= m - R_AT[3] < parts:
            stage_along(m - R_AT[3])
        if m == R_AT[3] + 5:
            finish(0)
    finish(1)
    for copy in started:
        copy.wait_send()
    for u in range(units - BUFFERS, parts):
        sib_copies[u].wait_send()
    for h in range(NH):
        for src in order:
            for way in (1, -1):

                @pl.when(sends(src, way))
                def _(h=h, src=src, way=way):
                    hidden_hop(h, src, way).wait_send()
                    along(h, src, way).wait_send()

        @pl.when(at_end)
        def _(h=h):
            sum_across(h).wait_send()
            across_hop(pieces.at[h, z], h_send.at[h], h_recv.at[h]).wait_send()
            across_hop(held.at[h, z, w], z_send.at[h], z_recv.at[h]).wait_send()
            for i in (1, 2):
                sum_hop(h, near, near_target(i)).wait_send()

        @pl.when(jnp.logical_not(at_end))
        def _(h=h):
            for i in range(2):
                sum_hop(h, near, near_target(i)).wait_send()
            sum_hop(h, -near, near_target(3)).wait_send()


def hand_over(result_ref, fresh_ref, result_out, fresh_out):
    result_out[...] = result_ref[...]
    fresh_out[...] = fresh_ref[...]


def layer_by_copies(
    hidden, norm_gain, w_qkv, qk_gain, w_out, cache, lengths, placing, routes, gate_w, w_gu, w_down
):
    _, span, cols = hidden.shape
    width = cols * 4
    held, _, _, inner = w_gu.shape
    experts = held * 8
    hr, rb = span // NH, span // NH // 4
    units = 4 * NH
    half, full = jnp.bfloat16, jnp.float32
    vmem = pl.BlockSpec(memory_space=pltpu.VMEM)
    smem = pl.BlockSpec(memory_space=pltpu.SMEM)
    anywhere = pl.BlockSpec(memory_space=pl.ANY)
    dma = pltpu.SemaphoreType.DMA
    scratch = pltpu.VMEM
    result, fresh = pl.pallas_call(
        layer_kernel,
        out_shape=(
            jax.ShapeDtypeStruct((span, cols), half),
            jax.ShapeDtypeStruct((2, span, cols), half),
        ),
        in_specs=[smem] * 2 + [vmem] * 5 + [anywhere] * 5,
        out_specs=(vmem, vmem),
        scratch_shapes=[
            scratch((NH, 4, hr, cols), half),
            scratch((3, width, cols), half),
            scratch((2,) + cache.shape[2:], half),
            scratch(w_out.shape, half),
            scratch((2, RAW_ROWS, 2, inner), half),
            scratch((held, width, 2 * inner), half),
            scratch((held * inner, width), half),
            scratch((2, span, HD), full),
            scratch((8, experts, span), full),
            scratch((128, span), full),
            scratch((span, 128), full),
            scratch((NH, 3, hr, cols), full),
            scratch((NH, hr, 128), full),
            scratch((NH, hr, cols), half),
            scratch((NH, 8, hr), full),
            scratch((NH, 4, 8, hr), full),
            scratch((NH, 4, rb, width), full),
            scratch((NH, 2, 4, rb, width), half),
            scratch((NH, 2, 4, rb, width), half),
            scratch((NH, rb, width), half),
            scratch((NH, 4, rb, cols), half),
            scratch((NH, 4, 8, rb, width), half),
            scratch((NH, 8, 4, rb, held * inner), half),
            scratch((BUFFERS, 4, hr, cols), half),
            scratch((units, 4, hr, cols), half),
            scratch((units, 2, hr, cols), half),
            scratch((KEEP, 2, hr, cols), full),
            scratch((units, 2, hr, cols), half),
            scratch((units, hr, cols), half),
            scratch((KEEP, hr, cols), full),
            scratch((units, hr, cols), half),
            scratch((units, hr, cols), half),
            scratch((units, hr, cols), half),
            scratch((NH, hr, cols), full),
            dma((4,)),
            dma((2,)),
            dma((NH, 2, 4)),
            dma((NH, 4)),
            dma((8,)),
            dma((8,)),
            dma((NH, 4)),
            dma((NH, 4)),
            dma((NH, 2, 4)),
            dma((NH, 2, 4)),
            dma((NH, 4)),
            dma((NH, 4)),
            dma((7 * units,)),
            dma((8, units)),
            dma((NH, 2, 4)),
            dma((NH, 4)),
            dma((4 * (units + TAIL_CUTS),)),
            dma((4 * (units + TAIL_CUTS),)),
        ],
        compiler_params=pltpu.CompilerParams(
            collective_id=0, has_side_effects=True, vmem_limit_bytes=VMEM_LIMIT
        ),
        name="layer",
    )(
        lengths,
        placing,
        hidden[0],
        norm_gain,
        qk_gain,
        jnp.transpose(routes[0]),
        jnp.transpose(gate_w[0]),
        jnp.transpose(w_qkv, (1, 0, 2)),
        cache[:, 0],
        w_out,
        w_gu,
        w_down.reshape(held * inner, width),
    )
    result, fresh = pl.pallas_call(
        hand_over,
        out_shape=(
            jax.ShapeDtypeStruct((span, cols), half),
            jax.ShapeDtypeStruct((2, span, cols), half),
        ),
        in_specs=[vmem] * 2,
        out_specs=(vmem, vmem),
        name="hand_over",
    )(result, fresh)
    return result[None], fresh[:, None]


def router_table(routes, gate_w, experts):
    named = routes[:, :, None] == jnp.arange(experts, dtype=jnp.int32)[None, None, :]
    return jnp.sum(jnp.where(named, gate_w[:, :, None], 0.0), axis=1)


def experts_by_collectives(after_rows, gain, routes, gate_w, w_gu, w_down):
    position = lax.axis_index("wide")
    column = lax.axis_index("narrow")
    wide_size = lax.axis_size("wide")
    narrow = lax.axis_size("narrow")
    rows, full_width = after_rows.shape
    span_len, share_cols = rows * narrow, full_width // narrow
    after_all = lax.all_gather(after_rows, ("wide", "narrow"), axis=0, tiled=True)
    after_own = lax.dynamic_slice(
        after_all, (position * span_len, column * share_cols), (span_len, share_cols)
    )
    routed = normalize(after_all, gain).astype(jnp.bfloat16)
    held_experts = w_gu.shape[0]
    inner_cols = w_gu.shape[3]
    experts = held_experts * wide_size
    table = router_table(routes, gate_w, experts)
    table = lax.all_gather(table, "wide", axis=0, tiled=True)
    scale = lax.dynamic_slice_in_dim(table, position * held_experts, held_experts, 1)
    pieces = []
    for j in range(held_experts):
        gate_up = jnp.dot(
            routed,
            w_gu[j].reshape(full_width, 2 * inner_cols),
            preferred_element_type=jnp.float32,
        )
        activated = jax.nn.silu(gate_up[:, :inner_cols]) * gate_up[:, inner_cols:]
        pieces.append((activated * scale[:, j : j + 1]).astype(jnp.bfloat16))
    weighted = jnp.concatenate(pieces, 1)
    combined = jnp.dot(
        weighted,
        w_down.reshape(held_experts * inner_cols, full_width),
        preferred_element_type=jnp.float32,
    ).astype(jnp.bfloat16)
    combined = lax.psum_scatter(combined, "wide", scatter_dimension=0, tiled=True)
    expert_out = lax.psum_scatter(
        combined, "narrow", scatter_dimension=1, tiled=True
    ).astype(jnp.float32)
    return (after_own.astype(jnp.float32) + expert_out).astype(jnp.bfloat16)

def per_device(
    hidden, norm_gain, w_qkv, qk_gain, w_out, cache, lengths, placing, routes, gate_w, w_gu, w_down
):
    narrow = lax.axis_size("narrow")
    column = lax.axis_index("narrow")
    position = lax.axis_index("wide")
    span_len = hidden.shape[1]
    share_cols = hidden.shape[2]
    full_width = share_cols * narrow
    tokens = lax.all_gather(hidden[0], "narrow", axis=1, tiled=True)
    normed = normalize(tokens, norm_gain[0]).astype(jnp.bfloat16)
    local_cols = w_qkv.shape[2]
    projected = jnp.dot(
        normed, w_qkv.reshape(full_width, 3 * local_cols), preferred_element_type=jnp.float32
    )
    queries = projected[:, :local_cols]
    keys_new = projected[:, local_cols : 2 * local_cols]
    values_new = projected[:, 2 * local_cols :]
    squares = lax.psum((jnp.sum(queries * queries, -1), jnp.sum(keys_new * keys_new, -1)), "narrow")
    features = local_cols * narrow
    queries = queries * lax.rsqrt(squares[0][:, None] / features + 1e-05) * qk_gain[0]
    keys_new = keys_new * lax.rsqrt(squares[1][:, None] / features + 1e-05) * qk_gain[1]
    head_count = local_cols // HD
    length = lengths[placing[position]]
    positions = length.astype(jnp.float32) + jnp.arange(span_len, dtype=jnp.float32)
    queries = rotary(queries.reshape(span_len, head_count, HD), positions).astype(jnp.bfloat16)
    keys_new = rotary(keys_new.reshape(span_len, head_count, HD), positions).astype(jnp.bfloat16)
    values_new = values_new.reshape(span_len, head_count, HD).astype(jnp.bfloat16)
    stored = cache.shape[2]
    all_keys = jnp.concatenate([cache[0, 0].reshape(stored, head_count, HD), keys_new], 0)
    all_values = jnp.concatenate([cache[1, 0].reshape(stored, head_count, HD), values_new], 0)
    scores = jnp.einsum(
        "thd,jhd->htj", queries, all_keys, preferred_element_type=jnp.float32
    ) * HD ** (-0.5)
    key_index = jnp.arange(stored + span_len, dtype=jnp.int32)[None, :]
    query_index = jnp.arange(span_len, dtype=jnp.int32)[:, None]
    allowed = jnp.where(key_index < stored, key_index < length, key_index - stored <= query_index)
    scores = jnp.where(allowed[None], scores, -1e30)
    highest = jnp.max(scores, axis=-1, keepdims=True)
    exponent = jnp.exp(scores - highest)
    weights = exponent.astype(jnp.bfloat16)
    denominator = jnp.sum(exponent, axis=-1)
    summed = jnp.einsum("htj,jhd->thd", weights, all_values, preferred_element_type=jnp.float32)
    heads_out = (
        (summed / jnp.transpose(denominator)[:, :, None])
        .astype(jnp.bfloat16)
        .reshape(span_len, local_cols)
    )
    partial_out = jnp.dot(heads_out, w_out, preferred_element_type=jnp.float32)
    rows = span_len // narrow
    attention = lax.psum_scatter(
        partial_out.astype(jnp.bfloat16), "narrow", scatter_dimension=0, tiled=True
    ).astype(jnp.float32)
    own_rows = lax.dynamic_slice_in_dim(tokens, column * rows, rows, 0)
    after_rows = (own_rows.astype(jnp.float32) + attention).astype(jnp.bfloat16)
    result = experts_by_collectives(
        after_rows, norm_gain[1], routes[0], gate_w[0], w_gu, w_down
    )[None]
    fresh = jnp.stack(
        [keys_new.reshape(span_len, local_cols), values_new.reshape(span_len, local_cols)]
    )[:, None]
    return (result, fresh)


def solution(mesh):
    placed = (
        P("wide", None, "narrow"),
        P(),
        P(None, None, "narrow"),
        P(None, "narrow"),
        P("narrow", None),
        P(None, "wide", None, "narrow"),
        P(),
        P(),
        P("wide", None, None),
        P("wide", None, None),
        P("wide", None, None, "narrow"),
        P("wide", "narrow", None),
    )
    by_copies = mesh.shape["wide"] == 8 and mesh.shape["narrow"] == 4
    return jax.shard_map(
        layer_by_copies if by_copies else per_device,
        mesh=mesh,
        in_specs=placed,
        out_specs=(P("wide", None, "narrow"), P(None, "wide", None, "narrow")),
        check_vma=False,
    )
```

```python
import math

import jax
import jax.numpy as jnp
from jax import lax
from jax.experimental import pallas as pl
from jax.experimental.pallas import tpu as pltpu
from jax.sharding import PartitionSpec as P

HD = 128


def normalize(values, gain_row):
    values = values.astype(jnp.float32)
    return (
        values
        * lax.rsqrt(jnp.mean(values * values, axis=-1, keepdims=True) + 1e-05)
        * gain_row.astype(jnp.float32)
    )


def rotary(values, positions):
    half_dim = values.shape[-1] // 2
    frequency = 10000.0 ** (-(jnp.arange(half_dim, dtype=jnp.float32) * (2.0 / values.shape[-1])))
    angle = positions[:, None] * frequency[None, :]
    cosine = jnp.cos(angle)[:, None, :]
    sine_part = jnp.sin(angle)[:, None, :]
    first_half = values[..., :half_dim]
    second_half = values[..., half_dim:]
    return jnp.concatenate(
        [
            first_half * cosine - second_half * sine_part,
            second_half * cosine + first_half * sine_part,
        ],
        axis=-1,
    )


NH = 2
BUFFERS = 4
RAW_ROWS = 1024
VMEM_LIMIT = 60 * 1024 * 1024
INVERSE = (0, 1, 2, 3, 4, 6, 5, 7)
EARLY_HEADS = 2
G_AT = (0, 1, 3, 4)
R_AT = (0, 1, 2, 3)
SUMS_AT = (0, 1, 2, 4)
KEEP = 2
TAIL_CUTS = 1
AFTER_AT = 13


def places():
    w = lax.axis_index("wide")
    z = lax.axis_index("narrow")
    c = lax.rem(w, 2)
    dx = 2 - 4 * lax.rem(lax.div(w, 2), 2)
    dy = 4 - 8 * lax.div(w, 4)
    first = dx * (1 - c) + dy * c
    second = dy * (1 - c) + dx * c
    return w, z, 1 - 2 * c, first, second


def layer_kernel(
    lengths_ref,
    placing_ref,
    hidden_ref,
    gain_ref,
    qk_gain_ref,
    routes_ref,
    gate_ref,
    w_qkv_any,
    cache_any,
    w_out_any,
    gu_any,
    down_any,
    out_ref,
    fresh_ref,
    pieces,
    w_qkv,
    cache,
    w_out,
    raw,
    gu,
    down,
    rope,
    gates_in,
    gate_rows,
    gate_cols,
    projected,
    squares,
    heads,
    stat_out,
    stat_in,
    partial,
    rs_out,
    rs_in,
    after,
    after_in,
    held,
    weighted,
    sib_out,
    sib_in,
    first_out,
    first_keep,
    first_in,
    second_out,
    second_keep,
    second_in,
    z_out,
    z_in,
    total,
    loads,
    raw_loads,
    h_send,
    h_recv,
    gates_send,
    gates_recv,
    stat_send,
    stat_recv,
    rs_send,
    rs_recv,
    after_send,
    after_recv,
    send,
    recv,
    z_send,
    z_recv,
    r_send,
    r_recv,
):
    w, z, sib, first, second = places()
    span, cols = hidden_ref.shape
    width = cols * 4
    hr = span // NH
    rb = hr // 4
    inner = gu.shape[2] // 2
    experts_held = gu.shape[0]
    steps = (
        0,
        first,
        second,
        first + second,
        sib,
        sib + second,
        sib + first,
        sib + first + second,
    )
    slots = [w + step for step in steps]
    upper = lax.div(z, 2)
    order = (z, z + 1 - 2 * lax.rem(z, 2), 2 - upper, 3 - 3 * upper)
    started = []

    def remote(src, dst, send_sem, recv_sem, device):
        return pltpu.make_async_remote_copy(
            src_ref=src,
            dst_ref=dst,
            send_sem=send_sem,
            recv_sem=recv_sem,
            device_id=device,
            device_id_type=pl.DeviceIdType.MESH,
        )

    def push(src, dst, send_sem, recv_sem, device):
        copy = remote(src, dst, send_sem, recv_sem, device)
        copy.start()
        started.append(copy)
        return copy

    def arrive(dst, recv_sem):
        remote(dst, dst, r_send.at[0], recv_sem, {"wide": w + sib}).wait_recv()

    load_qkv = pltpu.make_async_copy(w_qkv_any, w_qkv, loads.at[0])
    load_cache = pltpu.make_async_copy(cache_any, cache, loads.at[1])
    load_out = pltpu.make_async_copy(w_out_any, w_out, loads.at[2])
    load_down = pltpu.make_async_copy(down_any, down, loads.at[3])
    per_expert = width // RAW_ROWS
    chunks = experts_held * per_expert

    def load_raw(i):
        e, part = i // per_expert, i % per_expert
        return pltpu.make_async_copy(
            gu_any.at[e, pl.ds(part * RAW_ROWS, RAW_ROWS)], raw.at[i % 2], raw_loads.at[i % 2]
        )

    load_qkv.start()
    load_raw(0).start()
    load_raw(1).start()

    barrier = pltpu.get_barrier_semaphore()
    for step in steps[1:]:
        pl.semaphore_signal(
            barrier, inc=1, device_id={"wide": w + step}, device_id_type=pl.DeviceIdType.MESH
        )
    for k in (1, 2, 3):
        pl.semaphore_signal(
            barrier, inc=1, device_id={"narrow": order[k]}, device_id_type=pl.DeviceIdType.MESH
        )
    for h in range(NH):
        pieces[h, z] = hidden_ref[h * hr : (h + 1) * hr]
    pl.semaphore_wait(barrier, 10)

    def hop(buffer, send_sems, recv_sems, src, way):
        return remote(
            buffer,
            buffer,
            send_sems.at[(way + 1) // 2, src],
            recv_sems.at[src],
            {"narrow": lax.rem(z + way + 4, 4)},
        )

    def sends(src, way):
        if way > 0:
            return (src <= z) & (z < 3) & jnp.logical_not((src == 0) & (z == 2))
        return (src >= z) & (z > 0) & jnp.logical_not((src == 3) & (z == 1))

    low_half = z < 2
    near = jnp.where(low_half, 1, -1)
    at_end = (z == 0) | (z == 3)
    across_side = lax.div(1 - near, 2)

    def across_hop(buffer, send_sems, recv_sems):
        return remote(
            buffer, buffer, send_sems.at[across_side, z], recv_sems.at[z], {"narrow": 3 - z}
        )

    def hidden_hop(h, src, way):
        return hop(pieces.at[h, src], h_send.at[h], h_recv.at[h], src, way)

    def hidden_pass(h, src):
        for way in (1, -1):

            @pl.when(sends(src, way))
            def _(way=way):
                hidden_hop(h, src, way).start()

    def hidden_begin(h):
        @pl.when(at_end)
        def _():
            across_hop(pieces.at[h, z], h_send.at[h], h_recv.at[h]).start()

        hidden_pass(h, z)

    hidden_begin(0)
    load_cache.start()
    load_out.start()
    load_down.start()

    expert = lax.broadcasted_iota(jnp.int32, gates_in.shape[1:], 0)
    table = jnp.zeros(gates_in.shape[1:], jnp.float32)
    for k in range(routes_ref.shape[0]):
        table = table + jnp.where(routes_ref[k : k + 1, :] == expert, gate_ref[k : k + 1, :], 0.0)
    gates_in[0] = table
    for r in range(1, 8):
        push(
            gates_in.at[0],
            gates_in.at[INVERSE[r]],
            gates_send.at[r],
            gates_recv.at[INVERSE[r]],
            {"wide": w + steps[r]},
        )

    length = lengths_ref[placing_ref[w]]
    lane = lax.broadcasted_iota(jnp.int32, (1, HD), 1)
    frequency = jnp.exp(
        lax.rem(lane, HD // 2).astype(jnp.float32) * (-2.0 / HD * math.log(10000.0))
    )
    positions = (length + lax.broadcasted_iota(jnp.int32, (span, 1), 0)).astype(jnp.float32)
    angle = positions * frequency
    rope[0] = jnp.cos(angle)
    rope[1] = jnp.sin(angle) * jnp.where(lane < HD // 2, -1.0, 1.0)

    def contribute(h, src, start):
        values = pieces[h, src].astype(jnp.float32)
        at = pl.ds(pl.multiple_of(src * cols, cols), cols)
        scaled = (values * gain_ref[0:1, at].astype(jnp.float32)).astype(jnp.bfloat16)
        square = jnp.sum(values * values, axis=1, keepdims=True)
        for i in range(3):
            term = jnp.dot(scaled, w_qkv[i, at, :], preferred_element_type=jnp.float32)
            projected[h, i] = term if start else projected[h, i] + term
        wide = jnp.broadcast_to(square, squares.shape[1:])
        squares[h] = wide if start else squares[h] + wide

    def hidden_step(h, k):
        arrive(pieces.at[h, order[k]], h_recv.at[h, order[k]])
        hidden_pass(h, order[k])
        contribute(h, order[k], False)

    load_qkv.wait()
    contribute(0, z, True)

    row = lax.broadcasted_iota(jnp.int32, (256, 256), 0)
    column = lax.broadcasted_iota(jnp.int32, (256, 256), 1)
    part_them = (column == jnp.where(row < 128, 2 * row, 2 * row - 255)).astype(jnp.bfloat16)

    def part_chunk(i):
        load_raw(i).wait()

        def part(n, carry):
            at = pl.ds(pl.multiple_of(n * 128, 128), 128)
            to = pl.ds(pl.multiple_of(i % per_expert * RAW_ROWS + n * 128, 128), 128)
            both = jnp.dot(
                part_them,
                raw[i % 2, at].reshape(256, inner),
                preferred_element_type=jnp.float32,
            ).astype(jnp.bfloat16)
            gu[i // per_expert, to, 0:inner] = both[:128]
            gu[i // per_expert, to, inner : 2 * inner] = both[128:]
            return carry

        lax.fori_loop(0, RAW_ROWS // 128, part, 0)
        if i + 2 < chunks:
            load_raw(i + 2).start()

    def stats_push(h):
        scale = lax.rsqrt(squares[h, :, :1] / width + 1e-05)
        for i in range(3):
            projected[h, i] = projected[h, i] * scale
        spot = lax.broadcasted_iota(jnp.int32, (hr, 128), 1)
        both = [
            jnp.sum(projected[h, i] * projected[h, i], axis=1, keepdims=True) for i in range(2)
        ]
        sums = jnp.where(spot == 0, both[0], jnp.where(spot == 1, both[1], 0.0))
        stat_out[h] = sums.T[:8]
        for k in (1, 2, 3):
            push(
                stat_out.at[h],
                stat_in.at[h, z],
                stat_send.at[h, k],
                stat_recv.at[h, z],
                {"narrow": order[k]},
            )
        fresh_ref[1, h * hr : (h + 1) * hr] = projected[h, 2].astype(jnp.bfloat16)

    def stats_finish(h):
        totals = stat_out[h]
        for k in (1, 2, 3):
            arrive(stat_in.at[h, order[k]], stat_recv.at[h, order[k]])
            totals = totals + stat_in[h, order[k]]
        turned = jnp.concatenate([totals, jnp.zeros((120, hr), jnp.float32)], 0).T
        scales = lax.rsqrt(turned / width + 1e-05)
        for i in range(2):
            projected[h, i] = projected[h, i] * scales[:, i : i + 1] * qk_gain_ref[i : i + 1, :]

    across = (((1,), (1,)), ((), ()))
    stored = cache.shape[1]
    exponent_scale = HD ** (-0.5) * math.log2(math.e)

    def attend(h, low, high):
        rows = slice(h * hr, (h + 1) * hr)
        seen = (h + 1) * hr
        old_allowed = lax.broadcasted_iota(jnp.int32, (1, stored), 1) < length
        new_allowed = lax.broadcasted_iota(jnp.int32, (hr, seen), 1) <= h * hr + (
            lax.broadcasted_iota(jnp.int32, (hr, seen), 0)
        )

        def head(n, carry):
            at = pl.ds(pl.multiple_of(n * HD, HD), HD)
            cosine, sine = rope[0, rows], rope[1, rows]

            def turned(i):
                values = projected[h, i, :, at]
                return (values * cosine + pltpu.roll(values, HD // 2, 1) * sine).astype(
                    jnp.bfloat16
                )

            query = turned(0)
            fresh_ref[0, rows, at] = turned(1)
            old = lax.dot_general(
                query, cache[0, :, at], across, preferred_element_type=jnp.float32
            )
            new = lax.dot_general(
                query, fresh_ref[0, :seen, at], across, preferred_element_type=jnp.float32
            )
            old = jnp.where(old_allowed, old, -1e30)
            new = jnp.where(new_allowed, new, -1e30)
            highest = jnp.maximum(
                jnp.max(old, axis=1, keepdims=True), jnp.max(new, axis=1, keepdims=True)
            )
            old = jnp.exp2((old - highest) * exponent_scale)
            new = jnp.exp2((new - highest) * exponent_scale)
            denominator = jnp.sum(old, axis=1, keepdims=True) + jnp.sum(
                new, axis=1, keepdims=True
            )
            summed = jnp.dot(
                old.astype(jnp.bfloat16), cache[1, :, at], preferred_element_type=jnp.float32
            ) + jnp.dot(
                new.astype(jnp.bfloat16),
                fresh_ref[1, :seen, at],
                preferred_element_type=jnp.float32,
            )
            heads[h, :, at] = (summed / denominator).astype(jnp.bfloat16)
            return carry

        lax.fori_loop(low, high, head, 0)

    count = cols // HD

    def project(h):
        def chunk(i, carry):
            at = pl.ds(pl.multiple_of(i * cols, cols), cols)
            partial[h, :, :, at] = jnp.dot(
                heads[h], w_out[:, at], preferred_element_type=jnp.float32
            ).reshape(4, rb, cols)
            return carry

        lax.fori_loop(0, width // cols, chunk, 0)

    def sum_hop(h, way, d):
        side = lax.div(way + 1, 2)
        return remote(
            rs_out.at[h, side, d],
            rs_in.at[h, side, d],
            rs_send.at[h, side, d],
            rs_recv.at[h, side, d],
            {"narrow": lax.rem(z + way + 4, 4)},
        )

    def sum_across(h):
        return remote(
            rs_out.at[h, across_side, 3 - z],
            rs_in.at[h, across_side, 3 - z],
            rs_send.at[h, across_side, 3 - z],
            rs_recv.at[h, across_side, 3 - z],
            {"narrow": 3 - z},
        )

    def near_target(i):
        return jnp.where(low_half, 3 - i, i)

    def sums_begin(h):
        d = near_target(0)
        side = jnp.where(at_end, across_side, lax.div(near + 1, 2))
        rs_out[h, side, d] = partial[h, d].astype(jnp.bfloat16)

        @pl.when(at_end)
        def _():
            sum_across(h).start()
            for i in (1, 2):
                to = near_target(i)
                rs_out[h, lax.div(near + 1, 2), to] = partial[h, to].astype(jnp.bfloat16)
                sum_hop(h, near, to).start()

        @pl.when(jnp.logical_not(at_end))
        def _():
            sum_hop(h, near, d).start()

    def sums_pass(h, way, d):
        @pl.when(jnp.logical_not(at_end))
        def _():
            side = lax.div(way + 1, 2)
            sum_hop(h, way, d).wait_recv()
            rs_out[h, side, d] = (partial[h, d] + rs_in[h, side, d].astype(jnp.float32)).astype(
                jnp.bfloat16
            )
            sum_hop(h, way, d).start()

    def sums_step(h, i):
        if i == 0:
            sums_pass(h, near, near_target(1))
        else:
            sums_pass(h, -near, near_target(3))

    def columns(k):
        return pl.ds(pl.multiple_of(lax.rem(z + k, 4) * cols, cols), cols)

    def finish_after(h):
        for side in range(2):
            arrive(rs_in.at[h, side, z], rs_recv.at[h, side, z])
        added = (
            partial[h, z]
            + rs_in[h, 0, z].astype(jnp.float32)
            + rs_in[h, 1, z].astype(jnp.float32)
        )
        own = pl.ds(pl.multiple_of(z * rb, rb), rb)
        tokens = jnp.concatenate([pieces[h, i, own, :] for i in range(4)], 1)
        rounded = (tokens.astype(jnp.float32) + added).astype(jnp.bfloat16)
        after[h] = rounded
        values = rounded.astype(jnp.float32)
        mean = jnp.mean(values * values, axis=1, keepdims=True)
        held[h, z, w] = (
            values * lax.rsqrt(mean + 1e-05) * gain_ref[1:2, :].astype(jnp.float32)
        ).astype(jnp.bfloat16)

    def after_push(h):
        for k in (1, 3, 2):
            push(
                after.at[h, :, columns(k)],
                after_in.at[h, k],
                after_send.at[h, k],
                after_recv.at[h, k],
                {"narrow": lax.rem(z + k, 4)},
            )

    def gate_columns():
        for r in range(1, 8):
            arrive(gates_in.at[r], gates_recv.at[r])
        gate_rows[...] = jnp.zeros_like(gate_rows)
        for r in range(8):
            for j in range(experts_held):
                at = r * experts_held + j
                gate_rows[at : at + 1, :] = jnp.sum(
                    jnp.where(expert == w * experts_held + j, gates_in[r], 0.0),
                    axis=0,
                    keepdims=True,
                )
        gate_cols[...] = gate_rows[...].T

    pushed = []

    def push_rows(slot, n, role, step):
        h, k = n // 4, n % 4
        ref = held.at[h, order[k], slot]
        push(ref, ref, send.at[len(pushed)], recv.at[role, n], {"wide": w + step})
        pushed.append(n)

    def arrive_rows(role, n):
        h, k = n // 4, n % 4
        arrive(held.at[h, order[k], slots[role]], recv.at[role, n])

    def along(h, src, way):
        return hop(held.at[h, src, w], z_send.at[h], z_recv.at[h], src, way)

    def pass_on(h, k):
        src = order[k]
        if k == 0:

            @pl.when(at_end)
            def _():
                across_hop(held.at[h, z, w], z_send.at[h], z_recv.at[h]).start()

        for way in (1, -1):

            @pl.when(sends(src, way))
            def _(way=way):
                along(h, src, way).start()

    def expert_rows(n):
        h, g = n // 4, order[n % 4]
        inputs = jnp.concatenate([held[h, g, slot] for slot in slots], 0)
        weights = gate_cols[pl.ds(pl.multiple_of(h * hr + g * rb, rb), rb), :]
        lanes = lax.broadcasted_iota(jnp.int32, weights.shape, 1)

        def one(j, carry):
            scale = jnp.concatenate(
                [
                    jnp.sum(
                        jnp.where(lanes == r * experts_held + j, weights, 0.0),
                        axis=1,
                        keepdims=True,
                    )
                    for r in range(8)
                ],
                0,
            )
            both = jnp.dot(inputs, gu[j], preferred_element_type=jnp.float32)
            gate = both[:, :inner]
            active = gate / (1.0 + jnp.exp(-gate)) * both[:, inner:] * scale
            weighted[h, :, g, :, pl.ds(pl.multiple_of(j * inner, inner), inner)] = active.astype(
                jnp.bfloat16
            ).reshape(8, rb, inner)
            return carry

        lax.fori_loop(0, experts_held, one, 0)

    turns = (2, 1, 3, 0)
    units = 4 * NH

    cuts = [(m, 0, cols) for m in range(units - 1)] + [
        (units - 1, c * (cols // TAIL_CUTS), cols // TAIL_CUTS) for c in range(TAIL_CUTS)
    ]
    parts = len(cuts)

    def product(u, low):
        m, start, size = cuts[u]
        h, k = m // 4, turns[m % 4]
        values = weighted[h, low : low + 4].reshape(4 * hr, experts_held * inner)
        at = pl.ds(pl.multiple_of(lax.rem(z + k, 4) * cols + start, size), size)
        return jnp.dot(values, down[:, at], preferred_element_type=jnp.float32).reshape(
            4, hr, size
        )

    sib_copies = {}

    def spot_of(u):
        m, start, size = cuts[u]
        return m, slice(start, start + size), pl.ds(start, size)

    def stage_sib(u):
        m, at, to = spot_of(u)
        if m >= BUFFERS and cuts[u][1] == 0:
            sib_copies[m - BUFFERS].wait_send()
        sib_out[m % BUFFERS, :, :, at] = product(u, 4).astype(jnp.bfloat16)
        copy = remote(
            sib_out.at[m % BUFFERS, :, :, to],
            sib_in.at[m, :, :, to],
            r_send.at[u],
            r_recv.at[u],
            {"wide": w + sib},
        )
        copy.start()
        sib_copies[u] = copy

    def stage_first(u):
        m, at, to = spot_of(u)
        value = product(u, 0)
        arrive(sib_in.at[m, :, :, to], r_recv.at[u])
        for spot, r in ((0, 1), (1, 3)):
            first_out[m, spot, :, at] = (
                value[r] + sib_in[m, r, :, at].astype(jnp.float32)
            ).astype(jnp.bfloat16)
        push(
            first_out.at[m, :, :, to],
            first_in.at[m, :, :, to],
            r_send.at[parts + u],
            r_recv.at[parts + u],
            {"wide": w + first},
        )
        for spot, r in ((0, 0), (1, 2)):
            first_keep[m % KEEP, spot, :, at] = value[r] + sib_in[m, r, :, at].astype(jnp.float32)

    def stage_second(u):
        m, at, to = spot_of(u)
        arrive(first_in.at[m, :, :, to], r_recv.at[parts + u])
        second_out[m, :, at] = (
            first_keep[m % KEEP, 1, :, at] + first_in[m, 1, :, at].astype(jnp.float32)
        ).astype(jnp.bfloat16)
        push(
            second_out.at[m, :, to],
            second_in.at[m, :, to],
            r_send.at[2 * parts + u],
            r_recv.at[2 * parts + u],
            {"wide": w + second},
        )
        second_keep[m % KEEP, :, at] = first_keep[m % KEEP, 0, :, at] + first_in[
            m, 0, :, at
        ].astype(jnp.float32)

    def stage_along(u):
        m, at, to = spot_of(u)
        h, k = m // 4, turns[m % 4]
        arrive(second_in.at[m, :, to], r_recv.at[2 * parts + u])
        value = second_keep[m % KEEP, :, at] + second_in[m, :, at].astype(jnp.float32)
        if k:
            z_out[m] = value.astype(jnp.bfloat16)
            push(
                z_out.at[m],
                z_in.at[m],
                r_send.at[3 * parts + m],
                r_recv.at[3 * parts + m],
                {"narrow": lax.rem(z + k, 4)},
            )
        else:
            total[h, :, at] = value

    def finish(h):
        for k in (1, 2, 3):
            arrive(after_in.at[h, k], after_recv.at[h, k])
        for m in range(4 * h, 4 * h + 3):
            arrive(z_in.at[m], r_recv.at[3 * parts + m])
            total[h] = total[h] + z_in[m].astype(jnp.float32)
        for k in range(4):
            group = lax.rem(z + 4 - k, 4)
            block = pl.ds(pl.multiple_of(group * rb, rb), rb)
            to = pl.ds(pl.multiple_of(h * hr + group * rb, rb), rb)
            own = after_in[h, k] if k else after[h, :, columns(0)]
            out_ref[to, :] = (total[h, block, :] + own.astype(jnp.float32)).astype(jnp.bfloat16)

    part_chunk(0)
    hidden_step(0, 1)
    hidden_step(0, 2)
    part_chunk(1)
    hidden_step(0, 3)
    stats_push(0)
    hidden_begin(1)
    contribute(1, z, True)
    stats_finish(0)
    load_cache.wait()
    attend(0, 0, EARLY_HEADS)
    hidden_step(1, 1)
    attend(0, EARLY_HEADS, count)
    load_out.wait()
    project(0)
    sums_begin(0)
    hidden_step(1, 2)
    sums_step(0, 0)
    hidden_step(1, 3)
    stats_push(1)
    sums_step(0, 1)
    stats_finish(1)
    attend(1, 0, EARLY_HEADS)
    finish_after(0)

    lead = 4 + G_AT[3]
    for t in range(lead + parts + R_AT[3]):
        if t == SUMS_AT[3]:
            finish_after(1)
        if t < units:
            h, k = t // 4, t % 4
            if k == 0:
                pass_on(h, 0)
            push_rows(w, t, 1, first)
            push_rows(w, t, 2, second)
            push_rows(w, t, 4, sib)
        n = t - G_AT[1]
        if 0 <= n < units:
            arrive_rows(1, n)
            push_rows(slots[1], n, 3, second)
            push_rows(slots[1], n, 5, sib)
            arrive_rows(2, n)
            push_rows(slots[2], n, 6, sib)
        n = t - G_AT[2]
        if 0 <= n < units:
            arrive_rows(3, n)
            push_rows(slots[3], n, 7, sib)
        if t < units and t % 4 < 3:
            h, k = t // 4, t % 4
            src = order[k + 1]
            arrive(held.at[h, src, w], z_recv.at[h, src])
            pass_on(h, k + 1)
        if t == SUMS_AT[0]:
            attend(1, EARLY_HEADS, count)
            project(1)
            sums_begin(1)
        for i in range(2):
            if t == SUMS_AT[1 + i]:
                sums_step(1, i)
        if t == 3:
            load_down.wait()
        if t in (1, 2):
            part_chunk(t + 1)
        if t == 2:
            gate_columns()
        if t == AFTER_AT:
            after_push(0)
            after_push(1)
        m = t - lead
        if 0 <= m - R_AT[0] < parts:
            stage_sib(m - R_AT[0])
        if 0 <= m - R_AT[1] < parts:
            stage_first(m - R_AT[1])
        n = t - G_AT[3]
        if 0 <= n < units:
            for role in (4, 5, 6, 7):
                arrive_rows(role, n)
            expert_rows(n)
        if 0 <= m - R_AT[2] < parts:
            stage_second(m - R_AT[2])
        if 0 <= m - R_AT[3] < parts:
            stage_along(m - R_AT[3])
        if m == R_AT[3] + 5:
            finish(0)
    finish(1)
    for copy in started:
        copy.wait_send()
    for u in range(units - BUFFERS, parts):
        sib_copies[u].wait_send()
    for h in range(NH):
        for src in order:
            for way in (1, -1):

                @pl.when(sends(src, way))
                def _(h=h, src=src, way=way):
                    hidden_hop(h, src, way).wait_send()
                    along(h, src, way).wait_send()

        @pl.when(at_end)
        def _(h=h):
            sum_across(h).wait_send()
            across_hop(pieces.at[h, z], h_send.at[h], h_recv.at[h]).wait_send()
            across_hop(held.at[h, z, w], z_send.at[h], z_recv.at[h]).wait_send()
            for i in (1, 2):
                sum_hop(h, near, near_target(i)).wait_send()

        @pl.when(jnp.logical_not(at_end))
        def _(h=h):
            for i in range(2):
                sum_hop(h, near, near_target(i)).wait_send()
            sum_hop(h, -near, near_target(3)).wait_send()


def hand_over(result_ref, fresh_ref, result_out, fresh_out):
    result_out[...] = result_ref[...]
    fresh_out[...] = fresh_ref[...]


def layer_by_copies(
    hidden, norm_gain, w_qkv, qk_gain, w_out, cache, lengths, placing, routes, gate_w, w_gu, w_down
):
    _, span, cols = hidden.shape
    width = cols * 4
    held, _, _, inner = w_gu.shape
    experts = held * 8
    hr, rb = span // NH, span // NH // 4
    units = 4 * NH
    half, full = jnp.bfloat16, jnp.float32
    vmem = pl.BlockSpec(memory_space=pltpu.VMEM)
    smem = pl.BlockSpec(memory_space=pltpu.SMEM)
    anywhere = pl.BlockSpec(memory_space=pl.ANY)
    dma = pltpu.SemaphoreType.DMA
    scratch = pltpu.VMEM
    result, fresh = pl.pallas_call(
        layer_kernel,
        out_shape=(
            jax.ShapeDtypeStruct((span, cols), half),
            jax.ShapeDtypeStruct((2, span, cols), half),
        ),
        in_specs=[smem] * 2 + [vmem] * 5 + [anywhere] * 5,
        out_specs=(vmem, vmem),
        scratch_shapes=[
            scratch((NH, 4, hr, cols), half),
            scratch((3, width, cols), half),
            scratch((2,) + cache.shape[2:], half),
            scratch(w_out.shape, half),
            scratch((2, RAW_ROWS, 2, inner), half),
            scratch((held, width, 2 * inner), half),
            scratch((held * inner, width), half),
            scratch((2, span, HD), full),
            scratch((8, experts, span), full),
            scratch((128, span), full),
            scratch((span, 128), full),
            scratch((NH, 3, hr, cols), full),
            scratch((NH, hr, 128), full),
            scratch((NH, hr, cols), half),
            scratch((NH, 8, hr), full),
            scratch((NH, 4, 8, hr), full),
            scratch((NH, 4, rb, width), full),
            scratch((NH, 2, 4, rb, width), half),
            scratch((NH, 2, 4, rb, width), half),
            scratch((NH, rb, width), half),
            scratch((NH, 4, rb, cols), half),
            scratch((NH, 4, 8, rb, width), half),
            scratch((NH, 8, 4, rb, held * inner), half),
            scratch((BUFFERS, 4, hr, cols), half),
            scratch((units, 4, hr, cols), half),
            scratch((units, 2, hr, cols), half),
            scratch((KEEP, 2, hr, cols), full),
            scratch((units, 2, hr, cols), half),
            scratch((units, hr, cols), half),
            scratch((KEEP, hr, cols), full),
            scratch((units, hr, cols), half),
            scratch((units, hr, cols), half),
            scratch((units, hr, cols), half),
            scratch((NH, hr, cols), full),
            dma((4,)),
            dma((2,)),
            dma((NH, 2, 4)),
            dma((NH, 4)),
            dma((8,)),
            dma((8,)),
            dma((NH, 4)),
            dma((NH, 4)),
            dma((NH, 2, 4)),
            dma((NH, 2, 4)),
            dma((NH, 4)),
            dma((NH, 4)),
            dma((7 * units,)),
            dma((8, units)),
            dma((NH, 2, 4)),
            dma((NH, 4)),
            dma((4 * (units + TAIL_CUTS),)),
            dma((4 * (units + TAIL_CUTS),)),
        ],
        compiler_params=pltpu.CompilerParams(
            collective_id=0, has_side_effects=True, vmem_limit_bytes=VMEM_LIMIT
        ),
        name="layer",
    )(
        lengths,
        placing,
        hidden[0],
        norm_gain,
        qk_gain,
        jnp.transpose(routes[0]),
        jnp.transpose(gate_w[0]),
        jnp.transpose(w_qkv, (1, 0, 2)),
        cache[:, 0],
        w_out,
        w_gu,
        w_down.reshape(held * inner, width),
    )
    result, fresh = pl.pallas_call(
        hand_over,
        out_shape=(
            jax.ShapeDtypeStruct((span, cols), half),
            jax.ShapeDtypeStruct((2, span, cols), half),
        ),
        in_specs=[vmem] * 2,
        out_specs=(vmem, vmem),
        name="hand_over",
    )(result, fresh)
    return result[None], fresh[:, None]


def router_table(routes, gate_w, experts):
    named = routes[:, :, None] == jnp.arange(experts, dtype=jnp.int32)[None, None, :]
    return jnp.sum(jnp.where(named, gate_w[:, :, None], 0.0), axis=1)


def experts_by_collectives(after_rows, gain, routes, gate_w, w_gu, w_down):
    position = lax.axis_index("wide")
    column = lax.axis_index("narrow")
    wide_size = lax.axis_size("wide")
    narrow = lax.axis_size("narrow")
    rows, full_width = after_rows.shape
    span_len, share_cols = rows * narrow, full_width // narrow
    after_all = lax.all_gather(after_rows, ("wide", "narrow"), axis=0, tiled=True)
    after_own = lax.dynamic_slice(
        after_all, (position * span_len, column * share_cols), (span_len, share_cols)
    )
    routed = normalize(after_all, gain).astype(jnp.bfloat16)
    held_experts = w_gu.shape[0]
    inner_cols = w_gu.shape[3]
    experts = held_experts * wide_size
    table = router_table(routes, gate_w, experts)
    table = lax.all_gather(table, "wide", axis=0, tiled=True)
    scale = lax.dynamic_slice_in_dim(table, position * held_experts, held_experts, 1)
    pieces = []
    for j in range(held_experts):
        gate_up = jnp.dot(
            routed,
            w_gu[j].reshape(full_width, 2 * inner_cols),
            preferred_element_type=jnp.float32,
        )
        activated = jax.nn.silu(gate_up[:, :inner_cols]) * gate_up[:, inner_cols:]
        pieces.append((activated * scale[:, j : j + 1]).astype(jnp.bfloat16))
    weighted = jnp.concatenate(pieces, 1)
    combined = jnp.dot(
        weighted,
        w_down.reshape(held_experts * inner_cols, full_width),
        preferred_element_type=jnp.float32,
    ).astype(jnp.bfloat16)
    combined = lax.psum_scatter(combined, "wide", scatter_dimension=0, tiled=True)
    expert_out = lax.psum_scatter(
        combined, "narrow", scatter_dimension=1, tiled=True
    ).astype(jnp.float32)
    return (after_own.astype(jnp.float32) + expert_out).astype(jnp.bfloat16)

def per_device(
    hidden, norm_gain, w_qkv, qk_gain, w_out, cache, lengths, placing, routes, gate_w, w_gu, w_down
):
    narrow = lax.axis_size("narrow")
    column = lax.axis_index("narrow")
    position = lax.axis_index("wide")
    span_len = hidden.shape[1]
    share_cols = hidden.shape[2]
    full_width = share_cols * narrow
    tokens = lax.all_gather(hidden[0], "narrow", axis=1, tiled=True)
    normed = normalize(tokens, norm_gain[0]).astype(jnp.bfloat16)
    local_cols = w_qkv.shape[2]
    projected = jnp.dot(
        normed, w_qkv.reshape(full_width, 3 * local_cols), preferred_element_type=jnp.float32
    )
    queries = projected[:, :local_cols]
    keys_new = projected[:, local_cols : 2 * local_cols]
    values_new = projected[:, 2 * local_cols :]
    squares = lax.psum((jnp.sum(queries * queries, -1), jnp.sum(keys_new * keys_new, -1)), "narrow")
    features = local_cols * narrow
    queries = queries * lax.rsqrt(squares[0][:, None] / features + 1e-05) * qk_gain[0]
    keys_new = keys_new * lax.rsqrt(squares[1][:, None] / features + 1e-05) * qk_gain[1]
    head_count = local_cols // HD
    length = lengths[placing[position]]
    positions = length.astype(jnp.float32) + jnp.arange(span_len, dtype=jnp.float32)
    queries = rotary(queries.reshape(span_len, head_count, HD), positions).astype(jnp.bfloat16)
    keys_new = rotary(keys_new.reshape(span_len, head_count, HD), positions).astype(jnp.bfloat16)
    values_new = values_new.reshape(span_len, head_count, HD).astype(jnp.bfloat16)
    stored = cache.shape[2]
    all_keys = jnp.concatenate([cache[0, 0].reshape(stored, head_count, HD), keys_new], 0)
    all_values = jnp.concatenate([cache[1, 0].reshape(stored, head_count, HD), values_new], 0)
    scores = jnp.einsum(
        "thd,jhd->htj", queries, all_keys, preferred_element_type=jnp.float32
    ) * HD ** (-0.5)
    key_index = jnp.arange(stored + span_len, dtype=jnp.int32)[None, :]
    query_index = jnp.arange(span_len, dtype=jnp.int32)[:, None]
    allowed = jnp.where(key_index < stored, key_index < length, key_index - stored <= query_index)
    scores = jnp.where(allowed[None], scores, -1e30)
    highest = jnp.max(scores, axis=-1, keepdims=True)
    exponent = jnp.exp(scores - highest)
    weights = exponent.astype(jnp.bfloat16)
    denominator = jnp.sum(exponent, axis=-1)
    summed = jnp.einsum("htj,jhd->thd", weights, all_values, preferred_element_type=jnp.float32)
    heads_out = (
        (summed / jnp.transpose(denominator)[:, :, None])
        .astype(jnp.bfloat16)
        .reshape(span_len, local_cols)
    )
    partial_out = jnp.dot(heads_out, w_out, preferred_element_type=jnp.float32)
    rows = span_len // narrow
    attention = lax.psum_scatter(
        partial_out.astype(jnp.bfloat16), "narrow", scatter_dimension=0, tiled=True
    ).astype(jnp.float32)
    own_rows = lax.dynamic_slice_in_dim(tokens, column * rows, rows, 0)
    after_rows = (own_rows.astype(jnp.float32) + attention).astype(jnp.bfloat16)
    result = experts_by_collectives(
        after_rows, norm_gain[1], routes[0], gate_w[0], w_gu, w_down
    )[None]
    fresh = jnp.stack(
        [keys_new.reshape(span_len, local_cols), values_new.reshape(span_len, local_cols)]
    )[:, None]
    return (result, fresh)


def solution(mesh):
    placed = (
        P("wide", None, "narrow"),
        P(),
        P(None, None, "narrow"),
        P(None, "narrow"),
        P("narrow", None),
        P(None, "wide", None, "narrow"),
        P(),
        P(),
        P("wide", None, None),
        P("wide", None, None),
        P("wide", None, None, "narrow"),
        P("wide", "narrow", None),
    )
    by_copies = mesh.shape["wide"] == 8 and mesh.shape["narrow"] == 4
    return jax.shard_map(
        layer_by_copies if by_copies else per_device,
        mesh=mesh,
        in_specs=placed,
        out_specs=(P("wide", None, "narrow"), P(None, "wide", None, "narrow")),
        check_vma=False,
    )
```

```python
import math

import jax
import jax.numpy as jnp
from jax import lax
from jax.experimental import pallas as pl
from jax.experimental.pallas import tpu as pltpu
from jax.sharding import PartitionSpec as P

HD = 128


def normalize(values, gain_row):
    values = values.astype(jnp.float32)
    return (
        values
        * lax.rsqrt(jnp.mean(values * values, axis=-1, keepdims=True) + 1e-05)
        * gain_row.astype(jnp.float32)
    )


def rotary(values, positions):
    half_dim = values.shape[-1] // 2
    frequency = 10000.0 ** (-(jnp.arange(half_dim, dtype=jnp.float32) * (2.0 / values.shape[-1])))
    angle = positions[:, None] * frequency[None, :]
    cosine = jnp.cos(angle)[:, None, :]
    sine_part = jnp.sin(angle)[:, None, :]
    first_half = values[..., :half_dim]
    second_half = values[..., half_dim:]
    return jnp.concatenate(
        [
            first_half * cosine - second_half * sine_part,
            second_half * cosine + first_half * sine_part,
        ],
        axis=-1,
    )


NH = 2
BUFFERS = 4
RAW_ROWS = 1024
VMEM_LIMIT = 60 * 1024 * 1024
INVERSE = (0, 1, 2, 3, 4, 6, 5, 7)
EARLY_HEADS = 2
G_AT = (0, 1, 3, 4)
R_AT = (0, 1, 2, 3)
SUMS_AT = (0, 1, 2, 4)
KEEP = 2
TAIL_CUTS = 1
AFTER_AT = 13


def places():
    w = lax.axis_index("wide")
    z = lax.axis_index("narrow")
    c = lax.rem(w, 2)
    dx = 2 - 4 * lax.rem(lax.div(w, 2), 2)
    dy = 4 - 8 * lax.div(w, 4)
    first = dx * (1 - c) + dy * c
    second = dy * (1 - c) + dx * c
    return w, z, 1 - 2 * c, first, second


def layer_kernel(
    lengths_ref,
    placing_ref,
    hidden_ref,
    gain_ref,
    qk_gain_ref,
    routes_ref,
    gate_ref,
    w_qkv_any,
    cache_any,
    w_out_any,
    gu_any,
    down_any,
    out_ref,
    fresh_ref,
    pieces,
    w_qkv,
    cache,
    w_out,
    raw,
    gu,
    down,
    rope,
    gates_in,
    gate_rows,
    gate_cols,
    projected,
    squares,
    heads,
    stat_out,
    stat_in,
    partial,
    rs_out,
    rs_in,
    after,
    after_in,
    held,
    weighted,
    sib_out,
    sib_in,
    first_out,
    first_keep,
    first_in,
    second_out,
    second_keep,
    second_in,
    z_out,
    z_in,
    total,
    loads,
    raw_loads,
    h_send,
    h_recv,
    gates_send,
    gates_recv,
    stat_send,
    stat_recv,
    rs_send,
    rs_recv,
    after_send,
    after_recv,
    send,
    recv,
    z_send,
    z_recv,
    r_send,
    r_recv,
):
    w, z, sib, first, second = places()
    span, cols = hidden_ref.shape
    width = cols * 4
    hr = span // NH
    rb = hr // 4
    inner = gu.shape[2] // 2
    experts_held = gu.shape[0]
    steps = (
        0,
        first,
        second,
        first + second,
        sib,
        sib + second,
        sib + first,
        sib + first + second,
    )
    slots = [w + step for step in steps]
    upper = lax.div(z, 2)
    order = (z, z + 1 - 2 * lax.rem(z, 2), 2 - upper, 3 - 3 * upper)
    started = []

    def remote(src, dst, send_sem, recv_sem, device):
        return pltpu.make_async_remote_copy(
            src_ref=src,
            dst_ref=dst,
            send_sem=send_sem,
            recv_sem=recv_sem,
            device_id=device,
            device_id_type=pl.DeviceIdType.MESH,
        )

    def push(src, dst, send_sem, recv_sem, device):
        copy = remote(src, dst, send_sem, recv_sem, device)
        copy.start()
        started.append(copy)
        return copy

    def arrive(dst, recv_sem):
        remote(dst, dst, r_send.at[0], recv_sem, {"wide": w + sib}).wait_recv()

    load_qkv = pltpu.make_async_copy(w_qkv_any, w_qkv, loads.at[0])
    load_cache = pltpu.make_async_copy(cache_any, cache, loads.at[1])
    load_out = pltpu.make_async_copy(w_out_any, w_out, loads.at[2])
    load_down = pltpu.make_async_copy(down_any, down, loads.at[3])
    per_expert = width // RAW_ROWS
    chunks = experts_held * per_expert

    def load_raw(i):
        e, part = i // per_expert, i % per_expert
        return pltpu.make_async_copy(
            gu_any.at[e, pl.ds(part * RAW_ROWS, RAW_ROWS)], raw.at[i % 2], raw_loads.at[i % 2]
        )

    load_qkv.start()
    load_raw(0).start()
    load_raw(1).start()

    barrier = pltpu.get_barrier_semaphore()
    for step in steps[1:]:
        pl.semaphore_signal(
            barrier, inc=1, device_id={"wide": w + step}, device_id_type=pl.DeviceIdType.MESH
        )
    for k in (1, 2, 3):
        pl.semaphore_signal(
            barrier, inc=1, device_id={"narrow": order[k]}, device_id_type=pl.DeviceIdType.MESH
        )
    for h in range(NH):
        pieces[h, z] = hidden_ref[h * hr : (h + 1) * hr]
    pl.semaphore_wait(barrier, 10)

    def hop(buffer, send_sems, recv_sems, src, way):
        return remote(
            buffer,
            buffer,
            send_sems.at[(way + 1) // 2, src],
            recv_sems.at[src],
            {"narrow": lax.rem(z + way + 4, 4)},
        )

    def sends(src, way):
        if way > 0:
            return (src <= z) & (z < 3) & jnp.logical_not((src == 0) & (z == 2))
        return (src >= z) & (z > 0) & jnp.logical_not((src == 3) & (z == 1))

    low_half = z < 2
    near = jnp.where(low_half, 1, -1)
    at_end = (z == 0) | (z == 3)
    across_side = lax.div(1 - near, 2)

    def across_hop(buffer, send_sems, recv_sems):
        return remote(
            buffer, buffer, send_sems.at[across_side, z], recv_sems.at[z], {"narrow": 3 - z}
        )

    def hidden_hop(h, src, way):
        return hop(pieces.at[h, src], h_send.at[h], h_recv.at[h], src, way)

    def hidden_pass(h, src):
        for way in (1, -1):

            @pl.when(sends(src, way))
            def _(way=way):
                hidden_hop(h, src, way).start()

    def hidden_begin(h):
        @pl.when(at_end)
        def _():
            across_hop(pieces.at[h, z], h_send.at[h], h_recv.at[h]).start()

        hidden_pass(h, z)

    hidden_begin(0)
    load_cache.start()
    load_out.start()
    load_down.start()

    expert = lax.broadcasted_iota(jnp.int32, gates_in.shape[1:], 0)
    table = jnp.zeros(gates_in.shape[1:], jnp.float32)
    for k in range(routes_ref.shape[0]):
        table = table + jnp.where(routes_ref[k : k + 1, :] == expert, gate_ref[k : k + 1, :], 0.0)
    gates_in[0] = table
    for r in range(1, 8):
        push(
            gates_in.at[0],
            gates_in.at[INVERSE[r]],
            gates_send.at[r],
            gates_recv.at[INVERSE[r]],
            {"wide": w + steps[r]},
        )

    length = lengths_ref[placing_ref[w]]
    lane = lax.broadcasted_iota(jnp.int32, (1, HD), 1)
    frequency = jnp.exp(
        lax.rem(lane, HD // 2).astype(jnp.float32) * (-2.0 / HD * math.log(10000.0))
    )
    positions = (length + lax.broadcasted_iota(jnp.int32, (span, 1), 0)).astype(jnp.float32)
    angle = positions * frequency
    rope[0] = jnp.cos(angle)
    rope[1] = jnp.sin(angle) * jnp.where(lane < HD // 2, -1.0, 1.0)

    def contribute(h, src, start):
        values = pieces[h, src].astype(jnp.float32)
        at = pl.ds(pl.multiple_of(src * cols, cols), cols)
        scaled = (values * gain_ref[0:1, at].astype(jnp.float32)).astype(jnp.bfloat16)
        square = jnp.sum(values * values, axis=1, keepdims=True)
        for i in range(3):
            term = jnp.dot(scaled, w_qkv[i, at, :], preferred_element_type=jnp.float32)
            projected[h, i] = term if start else projected[h, i] + term
        wide = jnp.broadcast_to(square, squares.shape[1:])
        squares[h] = wide if start else squares[h] + wide

    def hidden_step(h, k):
        arrive(pieces.at[h, order[k]], h_recv.at[h, order[k]])
        hidden_pass(h, order[k])
        contribute(h, order[k], False)

    load_qkv.wait()
    contribute(0, z, True)

    row = lax.broadcasted_iota(jnp.int32, (256, 256), 0)
    column = lax.broadcasted_iota(jnp.int32, (256, 256), 1)
    part_them = (column == jnp.where(row < 128, 2 * row, 2 * row - 255)).astype(jnp.bfloat16)

    def part_chunk(i):
        load_raw(i).wait()

        def part(n, carry):
            at = pl.ds(pl.multiple_of(n * 128, 128), 128)
            to = pl.ds(pl.multiple_of(i % per_expert * RAW_ROWS + n * 128, 128), 128)
            both = jnp.dot(
                part_them,
                raw[i % 2, at].reshape(256, inner),
                preferred_element_type=jnp.float32,
            ).astype(jnp.bfloat16)
            gu[i // per_expert, to, 0:inner] = both[:128]
            gu[i // per_expert, to, inner : 2 * inner] = both[128:]
            return carry

        lax.fori_loop(0, RAW_ROWS // 128, part, 0)
        if i + 2 < chunks:
            load_raw(i + 2).start()

    def stats_push(h):
        scale = lax.rsqrt(squares[h, :, :1] / width + 1e-05)
        for i in range(3):
            projected[h, i] = projected[h, i] * scale
        spot = lax.broadcasted_iota(jnp.int32, (hr, 128), 1)
        both = [
            jnp.sum(projected[h, i] * projected[h, i], axis=1, keepdims=True) for i in range(2)
        ]
        sums = jnp.where(spot == 0, both[0], jnp.where(spot == 1, both[1], 0.0))
        stat_out[h] = sums.T[:8]
        for k in (1, 2, 3):
            push(
                stat_out.at[h],
                stat_in.at[h, z],
                stat_send.at[h, k],
                stat_recv.at[h, z],
                {"narrow": order[k]},
            )
        fresh_ref[1, h * hr : (h + 1) * hr] = projected[h, 2].astype(jnp.bfloat16)

    def stats_finish(h):
        totals = stat_out[h]
        for k in (1, 2, 3):
            arrive(stat_in.at[h, order[k]], stat_recv.at[h, order[k]])
            totals = totals + stat_in[h, order[k]]
        turned = jnp.concatenate([totals, jnp.zeros((120, hr), jnp.float32)], 0).T
        scales = lax.rsqrt(turned / width + 1e-05)
        for i in range(2):
            projected[h, i] = projected[h, i] * scales[:, i : i + 1] * qk_gain_ref[i : i + 1, :]

    across = (((1,), (1,)), ((), ()))
    stored = cache.shape[1]
    exponent_scale = HD ** (-0.5) * math.log2(math.e)

    def attend(h, low, high):
        rows = slice(h * hr, (h + 1) * hr)
        seen = (h + 1) * hr
        old_allowed = lax.broadcasted_iota(jnp.int32, (1, stored), 1) < length
        new_allowed = lax.broadcasted_iota(jnp.int32, (hr, seen), 1) <= h * hr + (
            lax.broadcasted_iota(jnp.int32, (hr, seen), 0)
        )

        def head(n, carry):
            at = pl.ds(pl.multiple_of(n * HD, HD), HD)
            cosine, sine = rope[0, rows], rope[1, rows]

            def turned(i):
                values = projected[h, i, :, at]
                return (values * cosine + pltpu.roll(values, HD // 2, 1) * sine).astype(
                    jnp.bfloat16
                )

            query = turned(0)
            fresh_ref[0, rows, at] = turned(1)
            old = lax.dot_general(
                query, cache[0, :, at], across, preferred_element_type=jnp.float32
            )
            new = lax.dot_general(
                query, fresh_ref[0, :seen, at], across, preferred_element_type=jnp.float32
            )
            old = jnp.where(old_allowed, old, -1e30)
            new = jnp.where(new_allowed, new, -1e30)
            highest = jnp.maximum(
                jnp.max(old, axis=1, keepdims=True), jnp.max(new, axis=1, keepdims=True)
            )
            old = jnp.exp2((old - highest) * exponent_scale)
            new = jnp.exp2((new - highest) * exponent_scale)
            denominator = jnp.sum(old, axis=1, keepdims=True) + jnp.sum(
                new, axis=1, keepdims=True
            )
            summed = jnp.dot(
                old.astype(jnp.bfloat16), cache[1, :, at], preferred_element_type=jnp.float32
            ) + jnp.dot(
                new.astype(jnp.bfloat16),
                fresh_ref[1, :seen, at],
                preferred_element_type=jnp.float32,
            )
            heads[h, :, at] = (summed / denominator).astype(jnp.bfloat16)
            return carry

        lax.fori_loop(low, high, head, 0)

    count = cols // HD

    def project(h):
        def chunk(i, carry):
            at = pl.ds(pl.multiple_of(i * cols, cols), cols)
            partial[h, :, :, at] = jnp.dot(
                heads[h], w_out[:, at], preferred_element_type=jnp.float32
            ).reshape(4, rb, cols)
            return carry

        lax.fori_loop(0, width // cols, chunk, 0)

    def sum_hop(h, way, d):
        side = lax.div(way + 1, 2)
        return remote(
            rs_out.at[h, side, d],
            rs_in.at[h, side, d],
            rs_send.at[h, side, d],
            rs_recv.at[h, side, d],
            {"narrow": lax.rem(z + way + 4, 4)},
        )

    def sum_across(h):
        return remote(
            rs_out.at[h, across_side, 3 - z],
            rs_in.at[h, across_side, 3 - z],
            rs_send.at[h, across_side, 3 - z],
            rs_recv.at[h, across_side, 3 - z],
            {"narrow": 3 - z},
        )

    def near_target(i):
        return jnp.where(low_half, 3 - i, i)

    def sums_begin(h):
        d = near_target(0)
        side = jnp.where(at_end, across_side, lax.div(near + 1, 2))
        rs_out[h, side, d] = partial[h, d].astype(jnp.bfloat16)

        @pl.when(at_end)
        def _():
            sum_across(h).start()
            for i in (1, 2):
                to = near_target(i)
                rs_out[h, lax.div(near + 1, 2), to] = partial[h, to].astype(jnp.bfloat16)
                sum_hop(h, near, to).start()

        @pl.when(jnp.logical_not(at_end))
        def _():
            sum_hop(h, near, d).start()

    def sums_pass(h, way, d):
        @pl.when(jnp.logical_not(at_end))
        def _():
            side = lax.div(way + 1, 2)
            sum_hop(h, way, d).wait_recv()
            rs_out[h, side, d] = (partial[h, d] + rs_in[h, side, d].astype(jnp.float32)).astype(
                jnp.bfloat16
            )
            sum_hop(h, way, d).start()

    def sums_step(h, i):
        if i == 0:
            sums_pass(h, near, near_target(1))
        else:
            sums_pass(h, -near, near_target(3))

    def columns(k):
        return pl.ds(pl.multiple_of(lax.rem(z + k, 4) * cols, cols), cols)

    def finish_after(h):
        for side in range(2):
            arrive(rs_in.at[h, side, z], rs_recv.at[h, side, z])
        added = (
            partial[h, z]
            + rs_in[h, 0, z].astype(jnp.float32)
            + rs_in[h, 1, z].astype(jnp.float32)
        )
        own = pl.ds(pl.multiple_of(z * rb, rb), rb)
        tokens = jnp.concatenate([pieces[h, i, own, :] for i in range(4)], 1)
        rounded = (tokens.astype(jnp.float32) + added).astype(jnp.bfloat16)
        after[h] = rounded
        values = rounded.astype(jnp.float32)
        mean = jnp.mean(values * values, axis=1, keepdims=True)
        held[h, z, w] = (
            values * lax.rsqrt(mean + 1e-05) * gain_ref[1:2, :].astype(jnp.float32)
        ).astype(jnp.bfloat16)

    def after_push(h):
        for k in (1, 3, 2):
            push(
                after.at[h, :, columns(k)],
                after_in.at[h, k],
                after_send.at[h, k],
                after_recv.at[h, k],
                {"narrow": lax.rem(z + k, 4)},
            )

    def gate_columns():
        for r in range(1, 8):
            arrive(gates_in.at[r], gates_recv.at[r])
        gate_rows[...] = jnp.zeros_like(gate_rows)
        for r in range(8):
            for j in range(experts_held):
                at = r * experts_held + j
                gate_rows[at : at + 1, :] = jnp.sum(
                    jnp.where(expert == w * experts_held + j, gates_in[r], 0.0),
                    axis=0,
                    keepdims=True,
                )
        gate_cols[...] = gate_rows[...].T

    pushed = []

    def push_rows(slot, n, role, step):
        h, k = n // 4, n % 4
        ref = held.at[h, order[k], slot]
        push(ref, ref, send.at[len(pushed)], recv.at[role, n], {"wide": w + step})
        pushed.append(n)

    def arrive_rows(role, n):
        h, k = n // 4, n % 4
        arrive(held.at[h, order[k], slots[role]], recv.at[role, n])

    def along(h, src, way):
        return hop(held.at[h, src, w], z_send.at[h], z_recv.at[h], src, way)

    def pass_on(h, k):
        src = order[k]
        if k == 0:

            @pl.when(at_end)
            def _():
                across_hop(held.at[h, z, w], z_send.at[h], z_recv.at[h]).start()

        for way in (1, -1):

            @pl.when(sends(src, way))
            def _(way=way):
                along(h, src, way).start()

    def expert_rows(n):
        h, g = n // 4, order[n % 4]
        inputs = jnp.concatenate([held[h, g, slot] for slot in slots], 0)
        weights = gate_cols[pl.ds(pl.multiple_of(h * hr + g * rb, rb), rb), :]
        lanes = lax.broadcasted_iota(jnp.int32, weights.shape, 1)

        def one(j, carry):
            scale = jnp.concatenate(
                [
                    jnp.sum(
                        jnp.where(lanes == r * experts_held + j, weights, 0.0),
                        axis=1,
                        keepdims=True,
                    )
                    for r in range(8)
                ],
                0,
            )
            both = jnp.dot(inputs, gu[j], preferred_element_type=jnp.float32)
            gate = both[:, :inner]
            active = gate / (1.0 + jnp.exp(-gate)) * both[:, inner:] * scale
            weighted[h, :, g, :, pl.ds(pl.multiple_of(j * inner, inner), inner)] = active.astype(
                jnp.bfloat16
            ).reshape(8, rb, inner)
            return carry

        lax.fori_loop(0, experts_held, one, 0)

    turns = (2, 1, 3, 0)
    units = 4 * NH

    cuts = [(m, 0, cols) for m in range(units - 1)] + [
        (units - 1, c * (cols // TAIL_CUTS), cols // TAIL_CUTS) for c in range(TAIL_CUTS)
    ]
    parts = len(cuts)

    def product(u, low):
        m, start, size = cuts[u]
        h, k = m // 4, turns[m % 4]
        values = weighted[h, low : low + 4].reshape(4 * hr, experts_held * inner)
        at = pl.ds(pl.multiple_of(lax.rem(z + k, 4) * cols + start, size), size)
        return jnp.dot(values, down[:, at], preferred_element_type=jnp.float32).reshape(
            4, hr, size
        )

    sib_copies = {}

    def spot_of(u):
        m, start, size = cuts[u]
        return m, slice(start, start + size), pl.ds(start, size)

    def stage_sib(u):
        m, at, to = spot_of(u)
        if m >= BUFFERS and cuts[u][1] == 0:
            sib_copies[m - BUFFERS].wait_send()
        sib_out[m % BUFFERS, :, :, at] = product(u, 4).astype(jnp.bfloat16)
        copy = remote(
            sib_out.at[m % BUFFERS, :, :, to],
            sib_in.at[m, :, :, to],
            r_send.at[u],
            r_recv.at[u],
            {"wide": w + sib},
        )
        copy.start()
        sib_copies[u] = copy

    def stage_first(u):
        m, at, to = spot_of(u)
        value = product(u, 0)
        arrive(sib_in.at[m, :, :, to], r_recv.at[u])
        for spot, r in ((0, 1), (1, 3)):
            first_out[m, spot, :, at] = (
                value[r] + sib_in[m, r, :, at].astype(jnp.float32)
            ).astype(jnp.bfloat16)
        push(
            first_out.at[m, :, :, to],
            first_in.at[m, :, :, to],
            r_send.at[parts + u],
            r_recv.at[parts + u],
            {"wide": w + first},
        )
        for spot, r in ((0, 0), (1, 2)):
            first_keep[m % KEEP, spot, :, at] = value[r] + sib_in[m, r, :, at].astype(jnp.float32)

    def stage_second(u):
        m, at, to = spot_of(u)
        arrive(first_in.at[m, :, :, to], r_recv.at[parts + u])
        second_out[m, :, at] = (
            first_keep[m % KEEP, 1, :, at] + first_in[m, 1, :, at].astype(jnp.float32)
        ).astype(jnp.bfloat16)
        push(
            second_out.at[m, :, to],
            second_in.at[m, :, to],
            r_send.at[2 * parts + u],
            r_recv.at[2 * parts + u],
            {"wide": w + second},
        )
        second_keep[m % KEEP, :, at] = first_keep[m % KEEP, 0, :, at] + first_in[
            m, 0, :, at
        ].astype(jnp.float32)

    def stage_along(u):
        m, at, to = spot_of(u)
        h, k = m // 4, turns[m % 4]
        arrive(second_in.at[m, :, to], r_recv.at[2 * parts + u])
        value = second_keep[m % KEEP, :, at] + second_in[m, :, at].astype(jnp.float32)
        if k:
            z_out[m] = value.astype(jnp.bfloat16)
            push(
                z_out.at[m],
                z_in.at[m],
                r_send.at[3 * parts + m],
                r_recv.at[3 * parts + m],
                {"narrow": lax.rem(z + k, 4)},
            )
        else:
            total[h, :, at] = value

    def finish(h):
        for k in (1, 2, 3):
            arrive(after_in.at[h, k], after_recv.at[h, k])
        for m in range(4 * h, 4 * h + 3):
            arrive(z_in.at[m], r_recv.at[3 * parts + m])
            total[h] = total[h] + z_in[m].astype(jnp.float32)
        for k in range(4):
            group = lax.rem(z + 4 - k, 4)
            block = pl.ds(pl.multiple_of(group * rb, rb), rb)
            to = pl.ds(pl.multiple_of(h * hr + group * rb, rb), rb)
            own = after_in[h, k] if k else after[h, :, columns(0)]
            out_ref[to, :] = (total[h, block, :] + own.astype(jnp.float32)).astype(jnp.bfloat16)

    part_chunk(0)
    hidden_step(0, 1)
    hidden_step(0, 2)
    part_chunk(1)
    hidden_step(0, 3)
    stats_push(0)
    hidden_begin(1)
    contribute(1, z, True)
    stats_finish(0)
    load_cache.wait()
    attend(0, 0, EARLY_HEADS)
    hidden_step(1, 1)
    attend(0, EARLY_HEADS, count)
    load_out.wait()
    project(0)
    sums_begin(0)
    hidden_step(1, 2)
    sums_step(0, 0)
    hidden_step(1, 3)
    stats_push(1)
    sums_step(0, 1)
    stats_finish(1)
    attend(1, 0, EARLY_HEADS)
    finish_after(0)

    lead = 4 + G_AT[3]
    for t in range(lead + parts + R_AT[3]):
        if t == SUMS_AT[3]:
            finish_after(1)
        if t < units:
            h, k = t // 4, t % 4
            if k == 0:
                pass_on(h, 0)
            push_rows(w, t, 1, first)
            push_rows(w, t, 2, second)
            push_rows(w, t, 4, sib)
        n = t - G_AT[1]
        if 0 <= n < units:
            arrive_rows(1, n)
            push_rows(slots[1], n, 3, second)
            push_rows(slots[1], n, 5, sib)
            arrive_rows(2, n)
            push_rows(slots[2], n, 6, sib)
        n = t - G_AT[2]
        if 0 <= n < units:
            arrive_rows(3, n)
            push_rows(slots[3], n, 7, sib)
        if t < units and t % 4 < 3:
            h, k = t // 4, t % 4
            src = order[k + 1]
            arrive(held.at[h, src, w], z_recv.at[h, src])
            pass_on(h, k + 1)
        if t == SUMS_AT[0]:
            attend(1, EARLY_HEADS, count)
            project(1)
            sums_begin(1)
        for i in range(2):
            if t == SUMS_AT[1 + i]:
                sums_step(1, i)
        if t == 3:
            load_down.wait()
        if t in (1, 2):
            part_chunk(t + 1)
        if t == 2:
            gate_columns()
        if t == AFTER_AT:
            after_push(0)
            after_push(1)
        m = t - lead
        if 0 <= m - R_AT[1] < parts:
            stage_first(m - R_AT[1])
        if 0 <= m - R_AT[0] < parts:
            stage_sib(m - R_AT[0])
        if 0 <= m - R_AT[2] < parts:
            stage_second(m - R_AT[2])
        if 0 <= m - R_AT[3] < parts:
            stage_along(m - R_AT[3])
        n = t - G_AT[3]
        if 0 <= n < units:
            for role in (4, 5, 6, 7):
                arrive_rows(role, n)
            expert_rows(n)
        if m == R_AT[3] + 5:
            finish(0)
    finish(1)
    for copy in started:
        copy.wait_send()
    for u in range(units - BUFFERS, parts):
        sib_copies[u].wait_send()
    for h in range(NH):
        for src in order:
            for way in (1, -1):

                @pl.when(sends(src, way))
                def _(h=h, src=src, way=way):
                    hidden_hop(h, src, way).wait_send()
                    along(h, src, way).wait_send()

        @pl.when(at_end)
        def _(h=h):
            sum_across(h).wait_send()
            across_hop(pieces.at[h, z], h_send.at[h], h_recv.at[h]).wait_send()
            across_hop(held.at[h, z, w], z_send.at[h], z_recv.at[h]).wait_send()
            for i in (1, 2):
                sum_hop(h, near, near_target(i)).wait_send()

        @pl.when(jnp.logical_not(at_end))
        def _(h=h):
            for i in range(2):
                sum_hop(h, near, near_target(i)).wait_send()
            sum_hop(h, -near, near_target(3)).wait_send()


def hand_over(result_ref, fresh_ref, result_out, fresh_out):
    result_out[...] = result_ref[...]
    fresh_out[...] = fresh_ref[...]


def layer_by_copies(
    hidden, norm_gain, w_qkv, qk_gain, w_out, cache, lengths, placing, routes, gate_w, w_gu, w_down
):
    _, span, cols = hidden.shape
    width = cols * 4
    held, _, _, inner = w_gu.shape
    experts = held * 8
    hr, rb = span // NH, span // NH // 4
    units = 4 * NH
    half, full = jnp.bfloat16, jnp.float32
    vmem = pl.BlockSpec(memory_space=pltpu.VMEM)
    smem = pl.BlockSpec(memory_space=pltpu.SMEM)
    anywhere = pl.BlockSpec(memory_space=pl.ANY)
    dma = pltpu.SemaphoreType.DMA
    scratch = pltpu.VMEM
    result, fresh = pl.pallas_call(
        layer_kernel,
        out_shape=(
            jax.ShapeDtypeStruct((span, cols), half),
            jax.ShapeDtypeStruct((2, span, cols), half),
        ),
        in_specs=[smem] * 2 + [vmem] * 5 + [anywhere] * 5,
        out_specs=(vmem, vmem),
        scratch_shapes=[
            scratch((NH, 4, hr, cols), half),
            scratch((3, width, cols), half),
            scratch((2,) + cache.shape[2:], half),
            scratch(w_out.shape, half),
            scratch((2, RAW_ROWS, 2, inner), half),
            scratch((held, width, 2 * inner), half),
            scratch((held * inner, width), half),
            scratch((2, span, HD), full),
            scratch((8, experts, span), full),
            scratch((128, span), full),
            scratch((span, 128), full),
            scratch((NH, 3, hr, cols), full),
            scratch((NH, hr, 128), full),
            scratch((NH, hr, cols), half),
            scratch((NH, 8, hr), full),
            scratch((NH, 4, 8, hr), full),
            scratch((NH, 4, rb, width), full),
            scratch((NH, 2, 4, rb, width), half),
            scratch((NH, 2, 4, rb, width), half),
            scratch((NH, rb, width), half),
            scratch((NH, 4, rb, cols), half),
            scratch((NH, 4, 8, rb, width), half),
            scratch((NH, 8, 4, rb, held * inner), half),
            scratch((BUFFERS, 4, hr, cols), half),
            scratch((units, 4, hr, cols), half),
            scratch((units, 2, hr, cols), half),
            scratch((KEEP, 2, hr, cols), full),
            scratch((units, 2, hr, cols), half),
            scratch((units, hr, cols), half),
            scratch((KEEP, hr, cols), full),
            scratch((units, hr, cols), half),
            scratch((units, hr, cols), half),
            scratch((units, hr, cols), half),
            scratch((NH, hr, cols), full),
            dma((4,)),
            dma((2,)),
            dma((NH, 2, 4)),
            dma((NH, 4)),
            dma((8,)),
            dma((8,)),
            dma((NH, 4)),
            dma((NH, 4)),
            dma((NH, 2, 4)),
            dma((NH, 2, 4)),
            dma((NH, 4)),
            dma((NH, 4)),
            dma((7 * units,)),
            dma((8, units)),
            dma((NH, 2, 4)),
            dma((NH, 4)),
            dma((4 * (units + TAIL_CUTS),)),
            dma((4 * (units + TAIL_CUTS),)),
        ],
        compiler_params=pltpu.CompilerParams(
            collective_id=0, has_side_effects=True, vmem_limit_bytes=VMEM_LIMIT
        ),
        name="layer",
    )(
        lengths,
        placing,
        hidden[0],
        norm_gain,
        qk_gain,
        jnp.transpose(routes[0]),
        jnp.transpose(gate_w[0]),
        jnp.transpose(w_qkv, (1, 0, 2)),
        cache[:, 0],
        w_out,
        w_gu,
        w_down.reshape(held * inner, width),
    )
    result, fresh = pl.pallas_call(
        hand_over,
        out_shape=(
            jax.ShapeDtypeStruct((span, cols), half),
            jax.ShapeDtypeStruct((2, span, cols), half),
        ),
        in_specs=[vmem] * 2,
        out_specs=(vmem, vmem),
        name="hand_over",
    )(result, fresh)
    return result[None], fresh[:, None]


def router_table(routes, gate_w, experts):
    named = routes[:, :, None] == jnp.arange(experts, dtype=jnp.int32)[None, None, :]
    return jnp.sum(jnp.where(named, gate_w[:, :, None], 0.0), axis=1)


def experts_by_collectives(after_rows, gain, routes, gate_w, w_gu, w_down):
    position = lax.axis_index("wide")
    column = lax.axis_index("narrow")
    wide_size = lax.axis_size("wide")
    narrow = lax.axis_size("narrow")
    rows, full_width = after_rows.shape
    span_len, share_cols = rows * narrow, full_width // narrow
    after_all = lax.all_gather(after_rows, ("wide", "narrow"), axis=0, tiled=True)
    after_own = lax.dynamic_slice(
        after_all, (position * span_len, column * share_cols), (span_len, share_cols)
    )
    routed = normalize(after_all, gain).astype(jnp.bfloat16)
    held_experts = w_gu.shape[0]
    inner_cols = w_gu.shape[3]
    experts = held_experts * wide_size
    table = router_table(routes, gate_w, experts)
    table = lax.all_gather(table, "wide", axis=0, tiled=True)
    scale = lax.dynamic_slice_in_dim(table, position * held_experts, held_experts, 1)
    pieces = []
    for j in range(held_experts):
        gate_up = jnp.dot(
            routed,
            w_gu[j].reshape(full_width, 2 * inner_cols),
            preferred_element_type=jnp.float32,
        )
        activated = jax.nn.silu(gate_up[:, :inner_cols]) * gate_up[:, inner_cols:]
        pieces.append((activated * scale[:, j : j + 1]).astype(jnp.bfloat16))
    weighted = jnp.concatenate(pieces, 1)
    combined = jnp.dot(
        weighted,
        w_down.reshape(held_experts * inner_cols, full_width),
        preferred_element_type=jnp.float32,
    ).astype(jnp.bfloat16)
    combined = lax.psum_scatter(combined, "wide", scatter_dimension=0, tiled=True)
    expert_out = lax.psum_scatter(
        combined, "narrow", scatter_dimension=1, tiled=True
    ).astype(jnp.float32)
    return (after_own.astype(jnp.float32) + expert_out).astype(jnp.bfloat16)

def per_device(
    hidden, norm_gain, w_qkv, qk_gain, w_out, cache, lengths, placing, routes, gate_w, w_gu, w_down
):
    narrow = lax.axis_size("narrow")
    column = lax.axis_index("narrow")
    position = lax.axis_index("wide")
    span_len = hidden.shape[1]
    share_cols = hidden.shape[2]
    full_width = share_cols * narrow
    tokens = lax.all_gather(hidden[0], "narrow", axis=1, tiled=True)
    normed = normalize(tokens, norm_gain[0]).astype(jnp.bfloat16)
    local_cols = w_qkv.shape[2]
    projected = jnp.dot(
        normed, w_qkv.reshape(full_width, 3 * local_cols), preferred_element_type=jnp.float32
    )
    queries = projected[:, :local_cols]
    keys_new = projected[:, local_cols : 2 * local_cols]
    values_new = projected[:, 2 * local_cols :]
    squares = lax.psum((jnp.sum(queries * queries, -1), jnp.sum(keys_new * keys_new, -1)), "narrow")
    features = local_cols * narrow
    queries = queries * lax.rsqrt(squares[0][:, None] / features + 1e-05) * qk_gain[0]
    keys_new = keys_new * lax.rsqrt(squares[1][:, None] / features + 1e-05) * qk_gain[1]
    head_count = local_cols // HD
    length = lengths[placing[position]]
    positions = length.astype(jnp.float32) + jnp.arange(span_len, dtype=jnp.float32)
    queries = rotary(queries.reshape(span_len, head_count, HD), positions).astype(jnp.bfloat16)
    keys_new = rotary(keys_new.reshape(span_len, head_count, HD), positions).astype(jnp.bfloat16)
    values_new = values_new.reshape(span_len, head_count, HD).astype(jnp.bfloat16)
    stored = cache.shape[2]
    all_keys = jnp.concatenate([cache[0, 0].reshape(stored, head_count, HD), keys_new], 0)
    all_values = jnp.concatenate([cache[1, 0].reshape(stored, head_count, HD), values_new], 0)
    scores = jnp.einsum(
        "thd,jhd->htj", queries, all_keys, preferred_element_type=jnp.float32
    ) * HD ** (-0.5)
    key_index = jnp.arange(stored + span_len, dtype=jnp.int32)[None, :]
    query_index = jnp.arange(span_len, dtype=jnp.int32)[:, None]
    allowed = jnp.where(key_index < stored, key_index < length, key_index - stored <= query_index)
    scores = jnp.where(allowed[None], scores, -1e30)
    highest = jnp.max(scores, axis=-1, keepdims=True)
    exponent = jnp.exp(scores - highest)
    weights = exponent.astype(jnp.bfloat16)
    denominator = jnp.sum(exponent, axis=-1)
    summed = jnp.einsum("htj,jhd->thd", weights, all_values, preferred_element_type=jnp.float32)
    heads_out = (
        (summed / jnp.transpose(denominator)[:, :, None])
        .astype(jnp.bfloat16)
        .reshape(span_len, local_cols)
    )
    partial_out = jnp.dot(heads_out, w_out, preferred_element_type=jnp.float32)
    rows = span_len // narrow
    attention = lax.psum_scatter(
        partial_out.astype(jnp.bfloat16), "narrow", scatter_dimension=0, tiled=True
    ).astype(jnp.float32)
    own_rows = lax.dynamic_slice_in_dim(tokens, column * rows, rows, 0)
    after_rows = (own_rows.astype(jnp.float32) + attention).astype(jnp.bfloat16)
    result = experts_by_collectives(
        after_rows, norm_gain[1], routes[0], gate_w[0], w_gu, w_down
    )[None]
    fresh = jnp.stack(
        [keys_new.reshape(span_len, local_cols), values_new.reshape(span_len, local_cols)]
    )[:, None]
    return (result, fresh)


def solution(mesh):
    placed = (
        P("wide", None, "narrow"),
        P(),
        P(None, None, "narrow"),
        P(None, "narrow"),
        P("narrow", None),
        P(None, "wide", None, "narrow"),
        P(),
        P(),
        P("wide", None, None),
        P("wide", None, None),
        P("wide", None, None, "narrow"),
        P("wide", "narrow", None),
    )
    by_copies = mesh.shape["wide"] == 8 and mesh.shape["narrow"] == 4
    return jax.shard_map(
        layer_by_copies if by_copies else per_device,
        mesh=mesh,
        in_specs=placed,
        out_specs=(P("wide", None, "narrow"), P(None, "wide", None, "narrow")),
        check_vma=False,
    )
```
